32 devices in a mesh: wall: 4 (over y, core), surf: 8 (over z, x).
Axes of the slice: x: 2, y: 2, z: 4, core: 2. Of those that a mesh axis runs over, the one named last changes fastest.
Arguments:
- vector: bfloat16 [32, 16, 320, 256], P('surf', 'wall'), may hold values from -40 to 40
- lengths: int32 [32], P('surf'), may hold values from 1 to 16, as said below
- north_of: int32 [8, 4], P('surf'), may hold values from 0 to 3, each once within a row
- diagonal: bfloat16 [32, 16, 320, 320], P('surf', 'wall'), may hold values from -1 to 8
- lifting: bfloat16 [32, 16, 6, 80, 320], P('surf', 'wall'), may hold values from -0.625 to 0.625
- inverse_rows: bfloat16 [32, 16, 80, 320], P('surf', 'wall'), may hold values from -0.25 to 0.25
Outputs:
- next_basis: bfloat16 [32, 16, 320, 256], P('surf', 'wall')
- coefs: float32 [2, 256], replicated
The draws below stay inside these ranges and needn't reach their ends.
Inputs may be any that keep to these rules, and one draw needn't show every extreme that they name: `lengths`: in every patch of 4 lines one line has 16 elements and another has 1.
All inputs are finite; a program needn't handle non-finite values.
Results may differ from the reference program's by a relative error of at most 0.00135.
Values may be sent and summed in bfloat16 or wider, within the bound.
A program may use at most 64 MiB of HBM per device.

```python
import math
import jax
import jax.numpy as jnp
from jax import lax

VARS = 5
NODE1D = 4
BLOCK = 320
FACE = 80
LINES_DEV = 4
R = 256
PATCHES = 8
LINES = 32
WALLPOS = 16


def draw_vector(key, part):
    subkeys = jax.random.split(key, 2)
    line_frac = jnp.arange(LINES, dtype=jnp.float32) / max(LINES - 1, 1)
    jitter = jnp.exp(jax.random.uniform(subkeys[0], (LINES, WALLPOS), jnp.float32, 0.0, math.log(3.3)))
    element_scale = 3.0 ** (line_frac[:, None] - 0.5) * jitter / 1.8
    noise = jax.random.truncated_normal(subkeys[1], -6.0, 6.0, (LINES, WALLPOS, BLOCK, R), jnp.float32)
    return (noise * element_scale[:, :, None, None]).astype(jnp.bfloat16)


def draw_diagonal(key, part):
    subkeys = jax.random.split(key, 2)
    wall_frac = jnp.arange(WALLPOS, dtype=jnp.float32) / max(WALLPOS - 1, 1)
    line_frac = jnp.arange(LINES, dtype=jnp.float32) / max(LINES - 1, 1)
    jitter = jnp.exp(jax.random.uniform(subkeys[0], (LINES, WALLPOS), jnp.float32, 0.0, math.log(1.5)))
    shift_term = 0.25 * 5.0 ** wall_frac[None, :] * 2.0 ** line_frac[:, None] * jitter
    offdiag = jax.random.truncated_normal(subkeys[1], -6.0, 6.0, (LINES, WALLPOS, BLOCK, BLOCK), jnp.float32)
    offdiag = offdiag / math.sqrt(BLOCK)
    unit_matrix = jnp.eye(BLOCK, dtype=jnp.float32)
    return (offdiag + shift_term[:, :, None, None] * unit_matrix).astype(jnp.bfloat16)


def draw_lengths(key, part):
    subkeys = jax.random.split(key, 3)
    baseline = jax.random.randint(subkeys[0], (PATCHES, LINES_DEV), 1, WALLPOS + 1)
    longest = jax.random.randint(subkeys[1], (PATCHES, 1), 0, LINES_DEV)
    shortest = (longest + 1 + jax.random.randint(subkeys[2], (PATCHES, 1), 0, LINES_DEV - 1)) % LINES_DEV
    slots = jnp.arange(LINES_DEV)[None, :]
    baseline = jnp.where(slots == longest, WALLPOS, baseline)
    baseline = jnp.where(slots == shortest, 1, baseline)
    return baseline.reshape(LINES).astype(jnp.int32)


def steps_of(key, dims, shards, smallest, high):
    def one(axis_at, parts):
        draws = jax.random.uniform(jax.random.fold_in(jax.random.fold_in(key, 6), axis_at), (parts,), jnp.float32, smallest / len(shards), high / len(shards))
        return jnp.repeat(jnp.exp(draws), dims[axis_at] // parts).reshape((-1,) + (1,) * (len(dims) - axis_at - 1))

    gain = one(*shards[0])
    for cut in shards[1:]:
        gain = gain * one(*cut)
    return gain


def scatter_about(rng, dims, scale, reach, cuts=(), held_as=jnp.bfloat16):
    values = scale * jax.random.normal(rng, dims, jnp.float32)
    if cuts:
        values = values * steps_of(rng, dims, cuts, -0.22, 0.18)
    return jnp.clip(values, -reach, reach).astype(held_as)


def setup_inputs(seed: int = 0) -> dict:
    streams_of = jax.random.split(jax.random.key(seed), 7)
    vector = draw_vector(jax.random.fold_in(streams_of[6], 71), 0)
    lengths = draw_lengths(jax.random.fold_in(streams_of[6], 71), 0)
    north_of = jax.vmap(lambda own: jax.random.permutation(own, LINES_DEV))(jax.random.split(streams_of[2], PATCHES)).reshape((PATCHES, LINES_DEV)).astype(jnp.int32)
    diagonal = draw_diagonal(jax.random.fold_in(streams_of[6], 71), 0)
    lifting = scatter_about(streams_of[4], (LINES, WALLPOS, 6, FACE, BLOCK), FACE ** -0.5, 0.625, ((0, 8), (1, 4)))
    inverse_rows = scatter_about(streams_of[5], (LINES, WALLPOS, FACE, BLOCK), (2 * BLOCK) ** -0.5, 0.25, ((0, 8), (1, 4)))
    return {"vector": vector, "lengths": lengths, "north_of": north_of, "diagonal": diagonal, "lifting": lifting, "inverse_rows": inverse_rows}


FULL_ACCURACY = lax.Precision.HIGHEST

def face_traces(values):
    leading = values.shape[:-2]
    column_entries = values.shape[-1]
    nodal_cube = values.reshape(leading + (VARS, NODE1D, NODE1D, NODE1D, column_entries))
    last_node = NODE1D - 1

    def flatten(piece):
        return piece.reshape(leading + (FACE, column_entries))
    bottom_face = flatten(nodal_cube[..., 0, :])
    top_face = flatten(nodal_cube[..., last_node, :])
    west_face = flatten(nodal_cube[..., 0, :, :, :])
    east_face = flatten(nodal_cube[..., last_node, :, :, :])
    south_face = flatten(nodal_cube[..., 0, :, :])
    north_face = flatten(nodal_cube[..., last_node, :, :])
    return (bottom_face, top_face, west_face, east_face, south_face, north_face)

def reference(vector, lengths, north_of, diagonal, lifting, inverse_rows):
    positions = jnp.arange(WALLPOS, dtype=jnp.int32)
    living = (positions[None, :] < lengths[:, None]).astype(jnp.float32)
    masked = vector * living[:, :, None, None].astype(jnp.bfloat16)
    bottom_face, top_face, west_face, east_face, south_face, north_face = face_traces(masked)
    zero_row = jnp.zeros_like(top_face[:, :1])
    from_below = jnp.concatenate([zero_row, top_face[:, :-1]], axis=1)
    from_above = jnp.concatenate([bottom_face[:, 1:], zero_row], axis=1)
    from_west = jnp.roll(east_face, 1, axis=0)
    from_east = jnp.roll(west_face, -1, axis=0)
    patch_base = (jnp.arange(PATCHES, dtype=jnp.int32) * LINES_DEV)[:, None]
    north_line = (patch_base + north_of).reshape(LINES).astype(jnp.int32)
    south_line = jnp.zeros((LINES,), jnp.int32).at[north_line].set(jnp.arange(LINES, dtype=jnp.int32))
    from_north = south_face[north_line]
    from_south = north_face[south_line]
    neighbours = jnp.stack([from_below, from_above, from_west, from_east, from_south, from_north], axis=2)

    def per_line(pieces):
        diagonal_row_block, lifted_line_term, inverse_line, line_under_mask, adjacent_line, living_line = pieces
        matrix_product = jnp.einsum('ont,oti->oni', diagonal_row_block.astype(jnp.float32), line_under_mask.astype(jnp.float32), precision=FULL_ACCURACY)
        matrix_product = matrix_product + jnp.einsum('ovih,ovip->ohp', lifted_line_term.astype(jnp.float32), adjacent_line.astype(jnp.float32), precision=FULL_ACCURACY)
        matrix_product = matrix_product * living_line[:, None, None]

        def advance(carried, inputs):
            product_now, lower_lift, inverse_now, alive_now = inputs
            eliminated = alive_now * (product_now - jnp.dot(lower_lift.T, carried, precision=FULL_ACCURACY))
            return (jnp.dot(inverse_now, eliminated, precision=FULL_ACCURACY), eliminated)
        start = jnp.zeros((FACE, R), jnp.float32)
        _, eliminated = lax.scan(advance, start, (matrix_product, lifted_line_term[:, 0].astype(jnp.float32), inverse_line.astype(jnp.float32), living_line))
        return eliminated
    eliminated = lax.map(per_line, (diagonal, lifting, inverse_rows, masked, neighbours, living))
    masked_wide = masked.astype(jnp.float32)
    coupling_total = lax.optimization_barrier(jnp.sum(masked_wide * eliminated, axis=(0, 1, 2)))
    self_sum = lax.optimization_barrier(jnp.sum(masked_wide * masked_wide, axis=(0, 1, 2)))
    projection = coupling_total / self_sum
    remainder = eliminated - projection * masked_wide
    entries = LINES * WALLPOS * BLOCK
    spread = jnp.sqrt(lax.optimization_barrier(jnp.sum(remainder * remainder, axis=(0, 1, 2))) / entries + 1e-06)
    next_basis = (remainder / spread).astype(jnp.bfloat16)
    coefs = jnp.stack([projection, spread])
    return (next_basis, coefs)
```

```python
import functools

import jax
import jax.numpy as jnp
from jax import lax
from jax.experimental import pallas as pl
from jax.experimental.pallas import tpu as pltpu
from jax.sharding import PartitionSpec as P

NODE1D = 4
F32 = jnp.float32
BF16 = jnp.bfloat16
MESH = pl.DeviceIdType.MESH


def times(a, b):
    return lax.dot_general(a, b, (((1,), (0,)), ((), ())), preferred_element_type=F32)


def left_t(a, b):
    return lax.dot_general(a, b, (((0,), (0,)), ((), ())), preferred_element_type=F32)


def right_t(a, b):
    return lax.dot_general(a, b, (((1,), (1,)), ((), ())), preferred_element_type=F32)


def split(x):
    high = x.astype(BF16)
    return high, (x - high.astype(F32)).astype(BF16)


def pack(x):
    high, low = split(x)
    return jnp.concatenate([high, high, low], axis=0)


def stack(x):
    high, low = split(x)
    return jnp.concatenate([high, low, high], axis=0)


def merge(gathered, count):
    p = [gathered[i, 0:1] for i in range(count)]
    s = [gathered[i, 1:2] for i in range(count)]
    o = [gathered[i, 2:3] for i in range(count)]
    r = [gathered[i, 3:4] for i in range(count)]
    total = sum(s[1:], s[0])
    cross = sum((o[i] + p[i] * s[i] for i in range(1, count)), o[0] + p[0] * s[0])
    safe = jnp.where(total > 0.0, total, 1.0)
    common = jnp.where(total > 0.0, cross / safe, 0.0)
    odd = jnp.zeros_like(total)
    square = jnp.zeros_like(total)
    for i in range(count):
        shift = p[i] - common
        odd = odd + (o[i] + shift * s[i])
        square = square + (r[i] + shift * (2.0 * o[i] + shift * s[i]))
    return common, total, odd, square, cross


def kernel(
    sizes, lengths, north_of, vector, diagonal, lifting, inverse, xv, prod, coefs,
    dg, lf, iv, xs, ts, top, bottom, south, north,
    below_in, above_in, west_in, east_in, at, mt, bt, vt, d, cf, ce, cin, cpack, cout,
    stat1, all1, stat2, all2,
    in_sem, halo_send, halo_recv, chain_send, chain_recv, s1_send, s1_recv, s2_send, s2_recv,
):
    lines, seg, block, face, cols, walls, surfs = sizes
    w = lax.axis_index("wall")
    s = lax.axis_index("surf")
    plane = NODE1D * NODE1D
    cube = plane * NODE1D
    outer = [0, lines - 1]
    inner = list(range(1, lines - 1))
    loads = []
    for n, (src, dst) in enumerate(((vector, xv), (inverse, iv), (lifting, lf), (diagonal, dg))):
        for l in range(lines):
            loads.append(pltpu.make_async_copy(src.at[l], dst.at[l], in_sem.at[n, l]))
    for copy in [loads[l] for l in outer + inner] + loads[lines:]:
        copy.start()
    barrier = pltpu.get_barrier_semaphore()
    for step in range(1, walls):
        pl.semaphore_signal(
            barrier, inc=1, device_id={"wall": lax.rem(w + step, walls)}, device_id_type=MESH
        )
    for step in range(1, surfs):
        pl.semaphore_signal(
            barrier, inc=1, device_id={"surf": lax.rem(s + step, surfs)}, device_id_type=MESH
        )

    def alive(l, k):
        return jnp.where(w * seg + k < lengths[l], 1.0, 0.0).astype(F32)

    def mask_line(l):
        def one(k, _):
            x = xv[l, k].astype(F32).reshape(block, cols) * alive(l, k)
            xv[l, k] = x.astype(BF16).reshape(xv.shape[2:])
            return 0

        loads[l].wait()
        lax.fori_loop(0, seg, one, 0)

    for l in outer:
        mask_line(l)
    pl.semaphore_wait(barrier, walls - 1 + surfs - 1)

    def remote(src, dst, send, recv, target):
        return pltpu.make_async_remote_copy(
            src_ref=src, dst_ref=dst, send_sem=send, recv_sem=recv,
            device_id=target, device_id_type=MESH,
        )

    to_east = remote(
        xv.at[lines - 1, :, :, cube - plane:cube], west_in, halo_send.at[0], halo_recv.at[0],
        {"surf": lax.rem(s + 1, surfs)},
    )
    to_west = remote(
        xv.at[0, :, :, 0:plane], east_in, halo_send.at[1], halo_recv.at[1],
        {"surf": lax.rem(s + surfs - 1, surfs)},
    )
    to_east.start()
    to_west.start()
    for l in inner:
        mask_line(l)

    count = block // plane

    def trace_one(i, _):
        l, k = i // seg, i % seg
        x = xv[l, k].astype(F32).reshape(block, cols)
        slot = lax.rem(i, 2)
        for h in range(cols // 128):
            xs[slot, h] = x[:, h * 128:(h + 1) * 128]
        for h in range(cols // 128):
            at_h = pl.ds(h * 128, 128)
            bottom[l, k, :, at_h] = xs[slot, h, pl.ds(0, face, stride=NODE1D), :].astype(BF16)
            top[l, k + 1, :, at_h] = xs[
                slot, h, pl.ds(NODE1D - 1, face, stride=NODE1D), :
            ].astype(BF16)
            for c in range(NODE1D):
                to = pl.ds(c, count, stride=NODE1D)
                ts[slot, h, 0, to, :] = xs[slot, h, pl.ds(c, count, stride=plane), :]
                ts[slot, h, 1, to, :] = xs[
                    slot, h, pl.ds(plane - NODE1D + c, count, stride=plane), :
                ]
        for h in range(cols // 128):
            at_h = pl.ds(h * 128, 128)
            south[l, k, :, at_h] = ts[slot, h, 0].astype(BF16)
            north[l, k, :, at_h] = ts[slot, h, 1].astype(BF16)
        return 0

    lax.fori_loop(0, lines * seg, trace_one, 0, unroll=2)

    up = {"wall": lax.rem(w + 1, walls)}
    down = {"wall": lax.rem(w + walls - 1, walls)}
    to_above = remote(top.at[:, seg], below_in, halo_send.at[2], halo_recv.at[2], up)
    to_below = remote(bottom.at[:, 0], above_in, halo_send.at[3], halo_recv.at[3], down)

    @pl.when(w < walls - 1)
    def _():
        to_above.start()

    @pl.when(w > 0)
    def _():
        to_below.start()

    row = lax.broadcasted_iota(jnp.int32, (face, face), 0)
    column = lax.broadcasted_iota(jnp.int32, (face, face), 1)
    eye = jnp.where(row == column, 1.0, 0.0).astype(F32)
    beyond = {0: 2 * face, lines - 1: 3 * face}

    for copy in loads[lines:3 * lines]:
        copy.wait()

    def map_one(k, _):
        for l in range(lines):
            a = (-alive(l, k)) * right_t(lf[l, k, 0:face], iv[l, k])
            at[l, k] = stack(a)
        for n, l in enumerate(outer):
            face_at = beyond[l]
            b = alive(l, k) * right_t(lf[l, k, face_at:face_at + face], iv[l, k])
            bt[n, k] = stack(b)
        return 0

    lax.fori_loop(0, seg, map_one, 0)

    def three(left, right):
        lh, ll = left[0:face], left[face:2 * face]
        rh, rl = right[0:face], right[face:2 * face]
        return times(lh, rh) + (times(ll, rh) + times(lh, rl))

    identity = stack(eye)
    for l in range(lines):
        mt[l, 0] = identity
        mt[l, 1] = at[l, 0]
    suffix = [identity for _ in outer]
    for n in range(len(outer)):
        vt[n, seg - 1] = bt[n, seg - 1, 0:2 * face]
    for k in range(1, seg):
        for l in range(lines):
            mt[l, k + 1] = stack(three(mt[l, k], at[l, k]))
        back = seg - k
        for n, l in enumerate(outer):
            suffix[n] = at[l, back] if k == 1 else stack(three(at[l, back], suffix[n]))
            vt[n, back - 1] = stack(three(bt[n, back - 1], suffix[n]))[0:2 * face]

    for copy in loads[3 * lines:]:
        copy.wait()

    south_of = []
    for l in range(lines):
        line = jnp.int32(0)
        for j in range(lines):
            line = jnp.where(north_of[0, j] == l, j, line)
        south_of.append(line)

    def fold(x):
        return jnp.sum(x.reshape(block // 8, 8, cols), axis=0)

    def local_step(k, acc):
        near, norm = acc
        for l in range(lines):
            x = xv[l, k].reshape(block, cols)
            sides = [top[l, k], bottom[l, k + 1]]
            if l > 0:
                sides.append(xv[l - 1, k, :, cube - plane:cube].reshape(face, cols))
            if l < lines - 1:
                sides.append(xv[l + 1, k, :, 0:plane].reshape(face, cols))
            sides += [north[south_of[l], k], south[north_of[0, l], k]]
            if l == 0:
                blocks = [lf[l, k, 0:2 * face], lf[l, k, 3 * face:6 * face]]
            elif l == lines - 1:
                blocks = [lf[l, k, 0:3 * face], lf[l, k, 4 * face:6 * face]]
            else:
                blocks = [lf[l, k]]
            p = times(dg[l, k], x) + left_t(
                jnp.concatenate(blocks, axis=0), jnp.concatenate(sides, axis=0)
            )
            p = alive(l, k) * p
            prod[l, k] = p
            high, low = split(p)
            d[l, k] = times(iv[l, k], high) + times(iv[l, k], low)
            wide = x.astype(F32)
            near = near + fold(wide * p)
            norm = norm + fold(wide * wide)
        return near, norm

    nothing = jnp.zeros((8, cols), F32)
    sums = lax.fori_loop(1, seg - 1, local_step, (nothing, nothing))

    @pl.when(w > 0)
    def _():
        to_above.wait_recv()
        for l in range(lines):
            top[l, 0] = below_in[l]

    @pl.when(w == 0)
    def _():
        for l in range(lines):
            top[l, 0] = jnp.zeros((face, cols), BF16)

    @pl.when(w < walls - 1)
    def _():
        to_below.wait_recv()
        for l in range(lines):
            bottom[l, seg] = above_in[l]

    @pl.when(w == walls - 1)
    def _():
        for l in range(lines):
            bottom[l, seg] = jnp.zeros((face, cols), BF16)

    near, norm = lax.fori_loop(
        0, 2, lambda i, acc: local_step(i * (seg - 1), acc), sums
    )

    chain = [
        remote(cout.at[l], cin.at[l], chain_send.at[l], chain_recv.at[l], up)
        for l in range(lines)
    ]

    def begin(group):
        @pl.when(w == 0)
        def _():
            for l in group:
                cout[l] = ce[l]
                chain[l].start()

    def take(group):
        for l in group:
            chain[l].wait_recv()
            cpack[l] = pack(cin[l])

            @pl.when(w < walls - 1)
            def _():
                cout[l] = ce[l] + left_t(mt[l, seg], cpack[l])
                chain[l].start()

    for l in range(lines):
        cf[l, 0] = jnp.zeros((face, cols), F32)
        cf[l, 1] = d[l, 0]
    for k in range(1, seg):
        for l in range(lines):
            c = d[l, k] + left_t(at[l, k], pack(cf[l, k]))
            if k < seg - 1:
                cf[l, k + 1] = c
            else:
                ce[l] = c
    begin(inner)

    halo = [west_in, east_in]
    to_east.wait_recv()
    to_west.wait_recv()
    for n, l in enumerate(outer):
        sides = [halo[n][k].reshape(face, cols) for k in range(seg)]
        ce[l] = ce[l] + left_t(
            vt[n].reshape(seg * 2 * face, face),
            jnp.concatenate([t for t in sides for _ in range(2)], axis=0),
        )
    begin(outer)

    @pl.when(w == 0)
    def _():
        cpack[...] = jnp.zeros_like(cpack)

    @pl.when(w == 1)
    def _():
        take(inner)
        take(outer)

    def late_one(k, _):
        for n, l in enumerate(outer):
            face_at = beyond[l]
            lower = lf[l, k, face_at:face_at + face]
            prod[l, k] += alive(l, k) * left_t(lower, halo[n][k].reshape(face, cols))
        return 0

    lax.fori_loop(0, seg, late_one, 0)
    late = [None for _ in outer]
    for k in range(seg - 1):
        for n, l in enumerate(outer):
            side = halo[n][k].reshape(face, cols)
            c = left_t(bt[n, k, 0:2 * face], jnp.concatenate([side, side], axis=0))
            if k > 0:
                c = c + left_t(at[l, k], pack(late[n]))
            late[n] = c
            cf[l, k + 1] += c

    near = jnp.sum(near, axis=0, keepdims=True)
    norm = jnp.sum(norm, axis=0, keepdims=True)
    guess = jnp.where(norm > 0.0, near / jnp.where(norm > 0.0, norm, 1.0), 0.0)

    def correct(group, k, acc):
        odd, square = acc
        for l in group:
            c = (-alive(l, k)) * (cf[l, k] + left_t(mt[l, k], cpack[l]))
            high, low = split(c)
            lower = lf[l, k, 0:face]
            e = prod[l, k] + left_t(
                jnp.concatenate([lower, lower], axis=0), jnp.concatenate([high, low], axis=0)
            )
            prod[l, k] = e
            x = xv[l, k].astype(F32).reshape(block, cols)
            e = e - guess * x
            odd = odd + fold(x * e)
            square = square + fold(e * e)
        return odd, square

    @pl.when(w > 1)
    def _():
        take(inner)

    sums = lax.fori_loop(
        0, seg, functools.partial(correct, inner), (nothing, nothing), unroll=2
    )

    @pl.when(w > 1)
    def _():
        take(outer)

    odd, square = lax.fori_loop(0, seg, functools.partial(correct, outer), sums, unroll=2)
    odd = jnp.sum(odd, axis=0, keepdims=True)
    square = jnp.sum(square, axis=0, keepdims=True)

    def gather(values, stat, slots, sends, recvs, axis, me, count):
        block_of = jnp.concatenate(list(values) + [jnp.zeros((4, cols), F32)], axis=0)
        stat[...] = block_of
        slots[me] = block_of
        copies = [
            remote(
                stat, slots.at[me], sends.at[d], recvs.at[d], {axis: lax.rem(me + d, count)}
            )
            for d in range(1, count)
        ]
        for copy in copies:
            copy.start()
        for copy in copies:
            copy.wait_recv()
        return copies

    sent1 = gather((guess, norm, odd, square), stat1, all1, s1_send, s1_recv, "wall", w, walls)
    common, total, odd, square, _ = merge(all1, walls)
    sent2 = gather((common, total, odd, square), stat2, all2, s2_send, s2_recv, "surf", s, surfs)
    _, total, _, square, cross = merge(all2, surfs)
    projection = cross / total
    entries = lines * seg * block * walls * surfs
    spread = jnp.sqrt(square / entries + 1e-06)
    coefs[0:1] = projection
    coefs[1:2] = spread
    for copy in sent1 + sent2 + [to_east, to_west]:
        copy.wait_send()

    @pl.when(w < walls - 1)
    def _():
        to_above.wait_send()
        for copy in chain:
            copy.wait_send()

    @pl.when(w > 0)
    def _():
        to_below.wait_send()


def finish(masked, eliminated, stats, basis, coefs):
    l = pl.program_id(0)
    coefs[...] = stats[...]
    projection = stats[0:1]
    scale = 1.0 / stats[1:2]
    for k in range(basis.shape[1]):
        x = masked[l, k].astype(F32).reshape(basis.shape[2:])
        basis[0, k] = ((eliminated[l, k] - projection * x) * scale).astype(BF16)


def per_device(walls, surfs, vector, lengths, north_of, diagonal, lifting, inverse_rows):
    lines, seg, block, cols = vector.shape
    face = inverse_rows.shape[2]
    sizes = (lines, seg, block, face, cols, walls, surfs)
    stacked = lifting.reshape(lines, seg, lifting.shape[2] * face, block)
    smem = pl.BlockSpec(memory_space=pltpu.SMEM)
    vmem = pl.BlockSpec(memory_space=pltpu.VMEM)
    hbm = pl.BlockSpec(memory_space=pltpu.HBM)
    dma = pltpu.SemaphoreType.DMA
    cubes = (lines, seg, block // NODE1D**3, NODE1D**3, cols)
    slab = (seg, block // NODE1D**3, NODE1D**2, cols)
    masked, eliminated, stats = pl.pallas_call(
        functools.partial(kernel, sizes),
        out_shape=(
            pltpu.VMEM(cubes, BF16),
            pltpu.VMEM(vector.shape, F32),
            pltpu.VMEM((2, cols), F32),
        ),
        in_specs=[smem, smem, hbm, hbm, hbm, hbm],
        out_specs=(vmem, vmem, vmem),
        scratch_shapes=[
            pltpu.VMEM(diagonal.shape, BF16),
            pltpu.VMEM(stacked.shape, BF16),
            pltpu.VMEM(inverse_rows.shape, BF16),
            pltpu.VMEM((2, cols // 128, block, 128), F32),
            pltpu.VMEM((2, cols // 128, 2, face, 128), F32),
            pltpu.VMEM((lines, seg + 1, face, cols), BF16),
            pltpu.VMEM((lines, seg + 1, face, cols), BF16),
            pltpu.VMEM((lines, seg, face, cols), BF16),
            pltpu.VMEM((lines, seg, face, cols), BF16),
            pltpu.VMEM((lines, face, cols), BF16),
            pltpu.VMEM((lines, face, cols), BF16),
            pltpu.VMEM(slab, BF16),
            pltpu.VMEM(slab, BF16),
            pltpu.VMEM((lines, seg, 3 * face, face), BF16),
            pltpu.VMEM((lines, seg + 1, 3 * face, face), BF16),
            pltpu.VMEM((2, seg, 3 * face, face), BF16),
            pltpu.VMEM((2, seg, 2 * face, face), BF16),
            pltpu.VMEM((lines, seg, face, cols), F32),
            pltpu.VMEM((lines, seg, face, cols), F32),
            pltpu.VMEM((lines, face, cols), F32),
            pltpu.VMEM((lines, face, cols), F32),
            pltpu.VMEM((lines, 3 * face, cols), BF16),
            pltpu.VMEM((lines, face, cols), F32),
            pltpu.VMEM((8, cols), F32),
            pltpu.VMEM((walls, 8, cols), F32),
            pltpu.VMEM((8, cols), F32),
            pltpu.VMEM((surfs, 8, cols), F32),
            dma((4, lines)),
            dma((4,)),
            dma((4,)),
            dma((lines,)),
            dma((lines,)),
            dma((walls,)),
            dma((walls,)),
            dma((surfs,)),
            dma((surfs,)),
        ],
        compiler_params=pltpu.CompilerParams(
            collective_id=0, has_side_effects=True, vmem_limit_bytes=56 * 1024 * 1024
        ),
    )(lengths, north_of, vector.reshape(cubes), diagonal, stacked, inverse_rows)
    return pl.pallas_call(
        finish,
        grid=(lines,),
        out_shape=(
            jax.ShapeDtypeStruct(vector.shape, BF16),
            jax.ShapeDtypeStruct((2, cols), F32),
        ),
        in_specs=[vmem, vmem, vmem],
        out_specs=(
            pl.BlockSpec((1, seg, block, cols), lambda l: (l, 0, 0, 0)),
            pl.BlockSpec((2, cols), lambda l: (0, 0)),
        ),
        compiler_params=pltpu.CompilerParams(vmem_limit_bytes=16 * 1024 * 1024),
    )(masked, eliminated, stats)


def solution(mesh):
    in_specs = (
        P("surf", "wall", None, None),
        P("surf"),
        P("surf", None),
        P("surf", "wall", None, None),
        P("surf", "wall", None, None, None),
        P("surf", "wall", None, None),
    )
    out_specs = (P("surf", "wall", None, None), P())
    return jax.shard_map(
        functools.partial(per_device, mesh.shape["wall"], mesh.shape["surf"]),
        mesh=mesh, in_specs=in_specs, out_specs=out_specs, check_vma=False,
    )
```

```python
import functools

import jax
import jax.numpy as jnp
from jax import lax
from jax.experimental import pallas as pl
from jax.experimental.pallas import tpu as pltpu
from jax.sharding import PartitionSpec as P

NODE1D = 4
F32 = jnp.float32
BF16 = jnp.bfloat16
MESH = pl.DeviceIdType.MESH


def times(a, b):
    return lax.dot_general(a, b, (((1,), (0,)), ((), ())), preferred_element_type=F32)


def left_t(a, b):
    return lax.dot_general(a, b, (((0,), (0,)), ((), ())), preferred_element_type=F32)


def right_t(a, b):
    return lax.dot_general(a, b, (((1,), (1,)), ((), ())), preferred_element_type=F32)


def split(x):
    high = x.astype(BF16)
    return high, (x - high.astype(F32)).astype(BF16)


def pack(x):
    high, low = split(x)
    return jnp.concatenate([high, high, low], axis=0)


def stack(x):
    high, low = split(x)
    return jnp.concatenate([high, low, high], axis=0)


def merge(gathered, count):
    p = [gathered[i, 0:1] for i in range(count)]
    s = [gathered[i, 1:2] for i in range(count)]
    o = [gathered[i, 2:3] for i in range(count)]
    r = [gathered[i, 3:4] for i in range(count)]
    total = sum(s[1:], s[0])
    cross = sum((o[i] + p[i] * s[i] for i in range(1, count)), o[0] + p[0] * s[0])
    safe = jnp.where(total > 0.0, total, 1.0)
    common = jnp.where(total > 0.0, cross / safe, 0.0)
    odd = jnp.zeros_like(total)
    square = jnp.zeros_like(total)
    for i in range(count):
        shift = p[i] - common
        odd = odd + (o[i] + shift * s[i])
        square = square + (r[i] + shift * (2.0 * o[i] + shift * s[i]))
    return common, total, odd, square, cross


def kernel(
    sizes, lengths, north_of, vector, diagonal, lifting, inverse, xv, prod, coefs,
    dg, lf, iv, xs, ts, top, bottom, south, north,
    below_in, above_in, west_in, east_in, at, mt, d, cf, ce, ck, cin, cpack, cout,
    stat1, all1, stat2, all2, final, final_in,
    in_sem, halo_send, halo_recv, chain_send, chain_recv,
    s1_send, s1_recv, s2_send, s2_recv, s3_send, s3_recv,
):
    lines, seg, block, face, cols, walls, surfs = sizes
    w = lax.axis_index("wall")
    s = lax.axis_index("surf")
    plane = NODE1D * NODE1D
    cube = plane * NODE1D
    outer = [0, lines - 1]
    inner = list(range(1, lines - 1))

    def load(n, src, dst):
        return [pltpu.make_async_copy(src(l), dst(l), in_sem.at[n, l]) for l in range(lines)]

    load_x = load(0, lambda l: vector.at[l], lambda l: xv.at[l])
    load_iv = load(1, lambda l: inverse.at[l], lambda l: iv.at[l])
    load_low = load(2, lambda l: lifting.at[l, :, 0:face], lambda l: lf.at[l, :, 0:face])
    rest = slice(face, 6 * face)
    load_lf = load(3, lambda l: lifting.at[l, :, rest], lambda l: lf.at[l, :, rest])
    load_dg = load(4, lambda l: diagonal.at[l], lambda l: dg.at[l])
    order = inner + outer
    for l in outer + inner:
        load_x[l].start()
    for l in order:
        load_iv[l].start()
        load_low[l].start()
    for l in order:
        load_lf[l].start()
        load_dg[l].start()
    barrier = pltpu.get_barrier_semaphore()
    for step in range(1, walls):
        pl.semaphore_signal(
            barrier, inc=1, device_id={"wall": lax.rem(w + step, walls)}, device_id_type=MESH
        )
    for step in range(1, surfs):
        pl.semaphore_signal(
            barrier, inc=1, device_id={"surf": lax.rem(s + step, surfs)}, device_id_type=MESH
        )

    def alive(l, k):
        return jnp.where(w * seg + k < lengths[l], 1.0, 0.0).astype(F32)

    def mask_line(l):
        def one(k, _):
            x = xv[l, k].astype(F32).reshape(block, cols) * alive(l, k)
            xv[l, k] = x.astype(BF16).reshape(xv.shape[2:])
            return 0

        load_x[l].wait()
        lax.fori_loop(0, seg, one, 0)

    for l in outer:
        mask_line(l)
    pl.semaphore_wait(barrier, walls - 1 + surfs - 1)

    def remote(src, dst, send, recv, target):
        return pltpu.make_async_remote_copy(
            src_ref=src, dst_ref=dst, send_sem=send, recv_sem=recv,
            device_id=target, device_id_type=MESH,
        )

    to_east = remote(
        xv.at[lines - 1, :, :, cube - plane:cube], west_in, halo_send.at[0], halo_recv.at[0],
        {"surf": lax.rem(s + 1, surfs)},
    )
    to_west = remote(
        xv.at[0, :, :, 0:plane], east_in, halo_send.at[1], halo_recv.at[1],
        {"surf": lax.rem(s + surfs - 1, surfs)},
    )
    to_east.start()
    for l in inner:
        mask_line(l)
    for l in order:
        load_iv[l].wait()
        load_low[l].wait()

    count = block // plane

    def trace_one(l, k, i):
        a = (-alive(l, k)) * right_t(lf[l, k, 0:face], iv[l, k])
        at[l, k] = stack(a)
        x = xv[l, k].astype(F32).reshape(block, cols)
        slot = lax.rem(i, 4)
        for h in range(cols // 128):
            xs[slot, h] = x[:, h * 128:(h + 1) * 128]
        for h in range(cols // 128):
            at_h = pl.ds(h * 128, 128)
            bottom[l, k, :, at_h] = xs[slot, h, pl.ds(0, face, stride=NODE1D), :].astype(BF16)
            top[l, k + 1, :, at_h] = xs[
                slot, h, pl.ds(NODE1D - 1, face, stride=NODE1D), :
            ].astype(BF16)
            for c in range(NODE1D):
                to = pl.ds(c, count, stride=NODE1D)
                ts[slot, h, 0, to, :] = xs[slot, h, pl.ds(c, count, stride=plane), :]
                ts[slot, h, 1, to, :] = xs[
                    slot, h, pl.ds(plane - NODE1D + c, count, stride=plane), :
                ]
        for h in range(cols // 128):
            at_h = pl.ds(h * 128, 128)
            south[l, k, :, at_h] = ts[slot, h, 0].astype(BF16)
            north[l, k, :, at_h] = ts[slot, h, 1].astype(BF16)

    def trace_ends(i, _):
        trace_one(i // 2, (i % 2) * (seg - 1), i)
        return 0

    def trace_rest(i, _):
        trace_one(i // (seg - 2), 1 + i % (seg - 2), i)
        return 0

    lax.fori_loop(0, 2 * lines, trace_ends, 0, unroll=2)

    up = {"wall": lax.rem(w + 1, walls)}
    down = {"wall": lax.rem(w + walls - 1, walls)}
    to_above = remote(top.at[:, seg], below_in, halo_send.at[2], halo_recv.at[2], up)
    to_below = remote(bottom.at[:, 0], above_in, halo_send.at[3], halo_recv.at[3], down)

    @pl.when(w < walls - 1)
    def _():
        to_above.start()

    @pl.when(w > 0)
    def _():
        to_below.start()

    lax.fori_loop(0, lines * (seg - 2), trace_rest, 0, unroll=2)
    to_east.wait_send()
    to_west.start()

    row = lax.broadcasted_iota(jnp.int32, (face, face), 0)
    column = lax.broadcasted_iota(jnp.int32, (face, face), 1)
    eye = jnp.where(row == column, 1.0, 0.0).astype(F32)

    def three(left, right):
        lh, ll = left[0:face], left[face:2 * face]
        rh, rl = right[0:face], right[face:2 * face]
        return times(lh, rh) + (times(ll, rh) + times(lh, rl))

    for l in range(lines):
        mt[l, 0] = stack(eye)
        mt[l, 1] = at[l, 0]
    for k in range(1, seg):
        for l in range(lines):
            mt[l, k + 1] = stack(three(mt[l, k], at[l, k]))

    south_of = []
    for l in range(lines):
        line = jnp.int32(0)
        for j in range(lines):
            line = jnp.where(north_of[0, j] == l, j, line)
        south_of.append(line)

    def fold(x):
        return jnp.sum(x.reshape(block // 8, 8, cols), axis=0)

    def local_step(group, k, acc):
        near, norm = acc
        for l in group:
            x = xv[l, k].reshape(block, cols)
            if l > 0:
                west = xv[l - 1, k, :, cube - plane:cube]
            else:
                west = west_in[k]
            if l < lines - 1:
                east = xv[l + 1, k, :, 0:plane]
            else:
                east = east_in[k]
            sides = [
                top[l, k], bottom[l, k + 1], west.reshape(face, cols), east.reshape(face, cols),
                north[south_of[l], k], south[north_of[0, l], k],
            ]
            p = times(dg[l, k], x) + left_t(lf[l, k], jnp.concatenate(sides, axis=0))
            p = alive(l, k) * p
            prod[l, k] = p
            wide = x.astype(F32)
            near = near + fold(wide * p)
            norm = norm + fold(wide * wide)
        return near, norm

    def inverse_step(group, k, _):
        for l in group:
            high, low = split(prod[l, k])
            d[l, k] = times(iv[l, k], high) + times(iv[l, k], low)
        return 0

    nothing = jnp.zeros((8, cols), F32)

    @pl.when(w > 0)
    def _():
        to_above.wait_recv()
        for l in range(lines):
            top[l, 0] = below_in[l]

    @pl.when(w == 0)
    def _():
        for l in range(lines):
            top[l, 0] = jnp.zeros((face, cols), BF16)

    @pl.when(w < walls - 1)
    def _():
        to_below.wait_recv()
        for l in range(lines):
            bottom[l, seg] = above_in[l]

    @pl.when(w == walls - 1)
    def _():
        for l in range(lines):
            bottom[l, seg] = jnp.zeros((face, cols), BF16)

    chain = [
        remote(cout.at[l], cin.at[l], chain_send.at[l], chain_recv.at[l], up)
        for l in range(lines)
    ]

    def begin(group):
        @pl.when(w == 0)
        def _():
            for l in group:
                cout[l] = ce[l]
                chain[l].start()

    def take(group):
        for l in group:
            chain[l].wait_recv()
            cpack[l] = pack(cin[l])

            @pl.when(w < walls - 1)
            def _():
                cout[l] = ce[l] + left_t(mt[l, seg], cpack[l])
                chain[l].start()

    def process(group, acc):
        for l in group:
            load_lf[l].wait()
            load_dg[l].wait()
        once = max(1, 4 // len(group))
        acc = lax.fori_loop(0, seg, functools.partial(local_step, group), acc, unroll=once)
        lax.fori_loop(0, seg, functools.partial(inverse_step, group), 0, unroll=4)
        for l in group:
            cf[l, 0] = jnp.zeros((face, cols), F32)
            cf[l, 1] = d[l, 0]
        for k in range(1, seg):
            for l in group:
                c = d[l, k] + left_t(at[l, k], pack(cf[l, k]))
                if k < seg - 1:
                    cf[l, k + 1] = c
                else:
                    ce[l] = c
        begin(group)
        return acc

    @pl.when(w == 0)
    def _():
        cpack[...] = jnp.zeros_like(cpack)

    sums = process(inner, (nothing, nothing))
    to_east.wait_recv()
    sums = process(outer[:1], sums)

    @pl.when(w == 1)
    def _():
        take(inner)

    to_west.wait_recv()
    near, norm = process(outer[1:], sums)

    @pl.when(w == 1)
    def _():
        take(outer)

    near = jnp.sum(near, axis=0, keepdims=True)
    norm = jnp.sum(norm, axis=0, keepdims=True)
    guess = jnp.where(norm > 0.0, near / jnp.where(norm > 0.0, norm, 1.0), 0.0)

    def carried(group, k, _):
        for l in group:
            c = (-alive(l, k)) * (cf[l, k] + left_t(mt[l, k], cpack[l]))
            high, low = split(c)
            ck[l, k, 0:face] = high
            ck[l, k, face:2 * face] = low
        return 0

    def correct_one(group, k, acc):
        odd, square = acc
        for l in group:
            lower = lf[l, k, 0:face]
            e = prod[l, k] + left_t(jnp.concatenate([lower, lower], axis=0), ck[l, k])
            prod[l, k] = e
            x = xv[l, k].astype(F32).reshape(block, cols)
            e = e - guess * x
            odd = odd + fold(x * e)
            square = square + fold(e * e)
        return odd, square

    def correct(group, acc):
        @pl.when(w > 1)
        def _():
            take(group)

        lax.fori_loop(0, seg, functools.partial(carried, group), 0, unroll=4)
        once = max(1, 4 // len(group))
        return lax.fori_loop(0, seg, functools.partial(correct_one, group), acc, unroll=once)

    sums = correct(inner, (nothing, nothing))
    sums = correct(outer[:1], sums)
    odd, square = correct(outer[1:], sums)
    odd = jnp.sum(odd, axis=0, keepdims=True)
    square = jnp.sum(square, axis=0, keepdims=True)

    last = walls - 1
    stat1[...] = jnp.concatenate(
        [guess, norm, odd, square, jnp.zeros((4, cols), F32)], axis=0
    )

    def to_last(i):
        return remote(stat1, all1.at[i], s1_send.at[0], s1_recv.at[i], {"wall": last})

    def to_peer(step):
        return remote(
            stat2, all2.at[s], s2_send.at[step], s2_recv.at[step],
            {"surf": lax.rem(s + step, surfs)},
        )

    def to_wall(i):
        return remote(final, final_in, s3_send.at[i], s3_recv.at[0], {"wall": i})

    @pl.when(w < last)
    def _():
        to_last(w).start()
        to_wall(0).wait_recv()
        coefs[...] = final_in[...]
        to_last(w).wait_send()

    @pl.when(w == last)
    def _():
        for i in range(last):
            to_last(i).wait_recv()
        all1[last] = stat1[...]
        common, total, odd, square, _ = merge(all1, walls)
        block_of = jnp.concatenate(
            [common, total, odd, square, jnp.zeros((4, cols), F32)], axis=0
        )
        stat2[...] = block_of
        all2[s] = block_of
        peers = [to_peer(step) for step in range(1, surfs)]
        for copy in peers:
            copy.start()
        for copy in peers:
            copy.wait_recv()
        _, total, _, square, cross = merge(all2, surfs)
        projection = cross / total
        entries = lines * seg * block * walls * surfs
        spread = jnp.sqrt(square / entries + 1e-06)
        result = jnp.concatenate([projection, spread], axis=0)
        final[...] = result
        for i in range(last):
            to_wall(i).start()
        coefs[...] = result
        for copy in peers:
            copy.wait_send()
        for i in range(last):
            to_wall(i).wait_send()

    to_west.wait_send()

    @pl.when(w < walls - 1)
    def _():
        to_above.wait_send()
        for copy in chain:
            copy.wait_send()

    @pl.when(w > 0)
    def _():
        to_below.wait_send()


def finish(masked, eliminated, stats, basis, coefs):
    l = pl.program_id(0)
    coefs[...] = stats[...]
    projection = stats[0:1]
    scale = 1.0 / stats[1:2]
    for k in range(basis.shape[1]):
        x = masked[l, k].astype(F32).reshape(basis.shape[2:])
        basis[0, k] = ((eliminated[l, k] - projection * x) * scale).astype(BF16)


def per_device(walls, surfs, vector, lengths, north_of, diagonal, lifting, inverse_rows):
    lines, seg, block, cols = vector.shape
    face = inverse_rows.shape[2]
    sizes = (lines, seg, block, face, cols, walls, surfs)
    stacked = lifting.reshape(lines, seg, lifting.shape[2] * face, block)
    smem = pl.BlockSpec(memory_space=pltpu.SMEM)
    vmem = pl.BlockSpec(memory_space=pltpu.VMEM)
    hbm = pl.BlockSpec(memory_space=pltpu.HBM)
    dma = pltpu.SemaphoreType.DMA
    cubes = (lines, seg, block // NODE1D**3, NODE1D**3, cols)
    slab = (seg, block // NODE1D**3, NODE1D**2, cols)
    masked, eliminated, stats = pl.pallas_call(
        functools.partial(kernel, sizes),
        out_shape=(
            pltpu.VMEM(cubes, BF16),
            pltpu.VMEM(vector.shape, F32),
            pltpu.VMEM((2, cols), F32),
        ),
        in_specs=[smem, smem, hbm, hbm, hbm, hbm],
        out_specs=(vmem, vmem, vmem),
        scratch_shapes=[
            pltpu.VMEM(diagonal.shape, BF16),
            pltpu.VMEM(stacked.shape, BF16),
            pltpu.VMEM(inverse_rows.shape, BF16),
            pltpu.VMEM((4, cols // 128, block, 128), F32),
            pltpu.VMEM((4, cols // 128, 2, face, 128), F32),
            pltpu.VMEM((lines, seg + 1, face, cols), BF16),
            pltpu.VMEM((lines, seg + 1, face, cols), BF16),
            pltpu.VMEM((lines, seg, face, cols), BF16),
            pltpu.VMEM((lines, seg, face, cols), BF16),
            pltpu.VMEM((lines, face, cols), BF16),
            pltpu.VMEM((lines, face, cols), BF16),
            pltpu.VMEM(slab, BF16),
            pltpu.VMEM(slab, BF16),
            pltpu.VMEM((lines, seg, 3 * face, face), BF16),
            pltpu.VMEM((lines, seg + 1, 3 * face, face), BF16),
            pltpu.VMEM((lines, seg, face, cols), F32),
            pltpu.VMEM((lines, seg, face, cols), F32),
            pltpu.VMEM((lines, face, cols), F32),
            pltpu.VMEM((lines, seg, 2 * face, cols), BF16),
            pltpu.VMEM((lines, face, cols), F32),
            pltpu.VMEM((lines, 3 * face, cols), BF16),
            pltpu.VMEM((lines, face, cols), F32),
            pltpu.VMEM((8, cols), F32),
            pltpu.VMEM((walls, 8, cols), F32),
            pltpu.VMEM((8, cols), F32),
            pltpu.VMEM((surfs, 8, cols), F32),
            pltpu.VMEM((2, cols), F32),
            pltpu.VMEM((2, cols), F32),
            dma((5, lines)),
            dma((4,)),
            dma((4,)),
            dma((lines,)),
            dma((lines,)),
            dma((1,)),
            dma((walls,)),
            dma((surfs,)),
            dma((surfs,)),
            dma((walls,)),
            dma((1,)),
        ],
        compiler_params=pltpu.CompilerParams(
            collective_id=0, has_side_effects=True, vmem_limit_bytes=56 * 1024 * 1024
        ),
    )(lengths, north_of, vector.reshape(cubes), diagonal, stacked, inverse_rows)
    return pl.pallas_call(
        finish,
        grid=(lines,),
        out_shape=(
            jax.ShapeDtypeStruct(vector.shape, BF16),
            jax.ShapeDtypeStruct((2, cols), F32),
        ),
        in_specs=[vmem, vmem, vmem],
        out_specs=(
            pl.BlockSpec((1, seg, block, cols), lambda l: (l, 0, 0, 0)),
            pl.BlockSpec((2, cols), lambda l: (0, 0)),
        ),
        compiler_params=pltpu.CompilerParams(vmem_limit_bytes=16 * 1024 * 1024),
    )(masked, eliminated, stats)


def solution(mesh):
    in_specs = (
        P("surf", "wall", None, None),
        P("surf"),
        P("surf", None),
        P("surf", "wall", None, None),
        P("surf", "wall", None, None, None),
        P("surf", "wall", None, None),
    )
    out_specs = (P("surf", "wall", None, None), P())
    return jax.shard_map(
        functools.partial(per_device, mesh.shape["wall"], mesh.shape["surf"]),
        mesh=mesh, in_specs=in_specs, out_specs=out_specs, check_vma=False,
    )
```

```python
import functools

import jax
import jax.numpy as jnp
from jax import lax
from jax.experimental import pallas as pl
from jax.experimental.pallas import tpu as pltpu
from jax.sharding import PartitionSpec as P

NODE1D = 4
F32 = jnp.float32
BF16 = jnp.bfloat16
MESH = pl.DeviceIdType.MESH


def times(a, b):
    return lax.dot_general(a, b, (((1,), (0,)), ((), ())), preferred_element_type=F32)


def left_t(a, b):
    return lax.dot_general(a, b, (((0,), (0,)), ((), ())), preferred_element_type=F32)


def right_t(a, b):
    return lax.dot_general(a, b, (((1,), (1,)), ((), ())), preferred_element_type=F32)


def split(x):
    high = x.astype(BF16)
    return high, (x - high.astype(F32)).astype(BF16)


def pack(x):
    high, low = split(x)
    return jnp.concatenate([high, high, low], axis=0)


def stack(x):
    high, low = split(x)
    return jnp.concatenate([high, low, high], axis=0)


def merge(gathered, count):
    p = [gathered[i, 0:1] for i in range(count)]
    s = [gathered[i, 1:2] for i in range(count)]
    o = [gathered[i, 2:3] for i in range(count)]
    r = [gathered[i, 3:4] for i in range(count)]
    total = sum(s[1:], s[0])
    cross = sum((o[i] + p[i] * s[i] for i in range(1, count)), o[0] + p[0] * s[0])
    safe = jnp.where(total > 0.0, total, 1.0)
    common = jnp.where(total > 0.0, cross / safe, 0.0)
    odd = jnp.zeros_like(total)
    square = jnp.zeros_like(total)
    for i in range(count):
        shift = p[i] - common
        odd = odd + (o[i] + shift * s[i])
        square = square + (r[i] + shift * (2.0 * o[i] + shift * s[i]))
    return common, total, odd, square, cross


def kernel(
    sizes, lengths, north_of, vector, diagonal, lifting, inverse, xv, prod, coefs,
    dg, lf, iv, xs, top, bottom, south, north,
    below_in, above_in, west_in, east_in, at, mt, d, cf, ce, ck, cin, cpack, cout,
    stat1, all1, stat2, all2, final, final_in,
    in_sem, halo_send, halo_recv, chain_send, chain_recv,
    s1_send, s1_recv, s2_send, s2_recv, s3_send, s3_recv,
):
    lines, seg, block, face, cols, walls, surfs = sizes
    w = lax.axis_index("wall")
    s = lax.axis_index("surf")
    plane = NODE1D * NODE1D
    cube = plane * NODE1D
    outer = [0, lines - 1]
    inner = list(range(1, lines - 1))

    groups = [inner, outer[:1], outer[1:]]
    load_x = pltpu.make_async_copy(vector, xv, in_sem.at[0, 0])
    load_iv = pltpu.make_async_copy(inverse, iv, in_sem.at[0, 1])
    load_lf, load_dg = [], []
    for n, group in enumerate(groups):
        part = slice(group[0], group[-1] + 1)
        load_lf.append(
            pltpu.make_async_copy(lifting.at[part], lf.at[part], in_sem.at[1, n])
        )
        load_dg.append(
            pltpu.make_async_copy(diagonal.at[part], dg.at[part], in_sem.at[2, n])
        )
    load_x.start()
    load_iv.start()
    for n in range(len(groups)):
        load_lf[n].start()
        load_dg[n].start()
    barrier = pltpu.get_barrier_semaphore()
    for step in range(1, walls):
        pl.semaphore_signal(
            barrier, inc=1, device_id={"wall": lax.rem(w + step, walls)}, device_id_type=MESH
        )
    for step in range(1, surfs):
        pl.semaphore_signal(
            barrier, inc=1, device_id={"surf": lax.rem(s + step, surfs)}, device_id_type=MESH
        )

    def alive(l, k):
        return jnp.where(w * seg + k < lengths[l], 1.0, 0.0).astype(F32)

    def mask_line(l):
        def one(k, _):
            x = xv[l, k].astype(F32).reshape(block, cols) * alive(l, k)
            xv[l, k] = x.astype(BF16).reshape(xv.shape[2:])
            return 0

        lax.fori_loop(0, seg, one, 0)

    load_x.wait()
    for l in outer:
        mask_line(l)
    pl.semaphore_wait(barrier, walls - 1 + surfs - 1)

    def remote(src, dst, send, recv, target):
        return pltpu.make_async_remote_copy(
            src_ref=src, dst_ref=dst, send_sem=send, recv_sem=recv,
            device_id=target, device_id_type=MESH,
        )

    to_east = remote(
        xv.at[lines - 1, :, :, cube - plane:cube], west_in, halo_send.at[0], halo_recv.at[0],
        {"surf": lax.rem(s + 1, surfs)},
    )
    to_west = remote(
        xv.at[0, :, :, 0:plane], east_in, halo_send.at[1], halo_recv.at[1],
        {"surf": lax.rem(s + surfs - 1, surfs)},
    )
    to_east.start()
    to_west.start()
    for l in inner:
        mask_line(l)

    count = block // plane

    def trace_one(l, k, i):
        x = xv[l, k].astype(F32).reshape(block, cols)
        slot = lax.rem(i, 4)
        for h in range(cols // 128):
            xs[slot, h] = x[:, h * 128:(h + 1) * 128]
        for h in range(cols // 128):
            at_h = pl.ds(h * 128, 128)
            bottom[l, k, :, at_h] = xs[slot, h, pl.ds(0, face, stride=NODE1D), :].astype(BF16)
            top[l, k + 1, :, at_h] = xs[
                slot, h, pl.ds(NODE1D - 1, face, stride=NODE1D), :
            ].astype(BF16)
        y = x.reshape(count, plane, cols)
        south[l, k] = y[:, 0:NODE1D].reshape(face, cols).astype(BF16)
        north[l, k] = y[:, plane - NODE1D:plane].reshape(face, cols).astype(BF16)

    def trace_ends(group, i, _):
        for l in group:
            trace_one(l, i * (seg - 1), 2 * i + group.index(l))
        return 0

    def trace_rest(i, _):
        trace_one(i // (seg - 2), 1 + i % (seg - 2), i)
        return 0


    up = {"wall": lax.rem(w + 1, walls)}
    down = {"wall": lax.rem(w + walls - 1, walls)}
    to_above, to_below = [], []
    for n, group in enumerate(groups):
        part = slice(group[0], group[-1] + 1)
        to_above.append(remote(
            top.at[part, seg], below_in.at[part], halo_send.at[2 + n], halo_recv.at[2 + n], up
        ))
        m = 2 + len(groups) + n
        to_below.append(remote(
            bottom.at[part, 0], above_in.at[part], halo_send.at[m], halo_recv.at[m], down
        ))

    def greet(parts):
        @pl.when(w < walls - 1)
        def _():
            for n in parts:
                to_above[n].start()

        @pl.when(w > 0)
        def _():
            for n in parts:
                to_below[n].start()

    lax.fori_loop(0, 2, functools.partial(trace_ends, inner), 0)
    greet([0])
    lax.fori_loop(0, 2, functools.partial(trace_ends, outer), 0)
    greet([1, 2])
    lax.fori_loop(0, lines * (seg - 2), trace_rest, 0, unroll=2)
    row = lax.broadcasted_iota(jnp.int32, (face, face), 0)
    column = lax.broadcasted_iota(jnp.int32, (face, face), 1)
    eye = jnp.where(row == column, 1.0, 0.0).astype(F32)

    def three(left, right):
        lh, ll = left[0:face], left[face:2 * face]
        rh, rl = right[0:face], right[face:2 * face]
        return times(lh, rh) + (times(ll, rh) + times(lh, rl))

    def map_one(group, k, _):
        for l in group:
            a = (-alive(l, k)) * right_t(lf[l, k, 0:face], iv[l, k])
            at[l, k] = stack(a)
        return 0

    load_iv.wait()
    for n, group in enumerate(groups):
        load_lf[n].wait()
        lax.fori_loop(0, seg, functools.partial(map_one, group), 0, unroll=4)

    @pl.when(w == 0)
    def _():
        mt[...] = jnp.zeros_like(mt)

    @pl.when(w > 0)
    def _():
        for l in range(lines):
            mt[l, 0] = stack(eye)
            mt[l, 1] = at[l, 0]
        for k in range(1, seg):
            for l in range(lines):
                mt[l, k + 1] = stack(three(mt[l, k], at[l, k]))

    south_of = []
    for l in range(lines):
        line = jnp.int32(0)
        for j in range(lines):
            line = jnp.where(north_of[0, j] == l, j, line)
        south_of.append(line)

    def fold(x):
        return jnp.sum(x.reshape(block // 8, 8, cols), axis=0)

    def local_step(group, k, acc):
        near, norm = acc
        for l in group:
            x = xv[l, k].reshape(block, cols)
            if l > 0:
                west = xv[l - 1, k, :, cube - plane:cube]
            else:
                west = west_in[k]
            if l < lines - 1:
                east = xv[l + 1, k, :, 0:plane]
            else:
                east = east_in[k]
            sides = [
                top[l, k], bottom[l, k + 1], west.reshape(face, cols), east.reshape(face, cols),
                north[south_of[l], k], south[north_of[0, l], k],
            ]
            p = times(dg[l, k], x) + left_t(lf[l, k], jnp.concatenate(sides, axis=0))
            p = alive(l, k) * p
            prod[l, k] = p
            wide = x.astype(F32)
            near = near + fold(wide * p)
            norm = norm + fold(wide * wide)
        return near, norm

    def inverse_step(group, k, _):
        for l in group:
            high, low = split(prod[l, k])
            d[l, k] = times(iv[l, k], high) + times(iv[l, k], low)
        return 0

    nothing = jnp.zeros((8, cols), F32)

    def meet(n):
        group = groups[n]

        @pl.when(w > 0)
        def _():
            to_above[n].wait_recv()
            for l in group:
                top[l, 0] = below_in[l]

        @pl.when(w == 0)
        def _():
            for l in group:
                top[l, 0] = jnp.zeros((face, cols), BF16)

        @pl.when(w < walls - 1)
        def _():
            to_below[n].wait_recv()
            for l in group:
                bottom[l, seg] = above_in[l]

        @pl.when(w == walls - 1)
        def _():
            for l in group:
                bottom[l, seg] = jnp.zeros((face, cols), BF16)

    chain = [
        remote(cout.at[l], cin.at[l], chain_send.at[l], chain_recv.at[l], up)
        for l in range(lines)
    ]

    def begin(group):
        @pl.when(w == 0)
        def _():
            for l in group:
                cout[l] = ce[l]
                chain[l].start()

    def take(group):
        for l in group:
            chain[l].wait_recv()
            cpack[l] = pack(cin[l])

            @pl.when(w < walls - 1)
            def _():
                cout[l] = ce[l] + left_t(mt[l, seg], cpack[l])
                chain[l].start()

    def process(n, acc):
        group = groups[n]
        load_dg[n].wait()
        once = max(1, 4 // len(group))
        meet(n)
        acc = lax.fori_loop(0, seg, functools.partial(local_step, group), acc, unroll=once)
        lax.fori_loop(0, seg, functools.partial(inverse_step, group), 0, unroll=4)
        for l in group:
            cf[l, 0] = jnp.zeros((face, cols), F32)
            cf[l, 1] = d[l, 0]
        for k in range(1, seg):
            for l in group:
                c = d[l, k] + left_t(at[l, k], pack(cf[l, k]))
                if k < seg - 1:
                    cf[l, k + 1] = c
                else:
                    ce[l] = c
        begin(group)
        return acc

    @pl.when(w == 0)
    def _():
        cpack[...] = jnp.zeros_like(cpack)

    sums = process(0, (nothing, nothing))
    to_east.wait_recv()
    sums = process(1, sums)

    @pl.when(w == 1)
    def _():
        take(inner)

    to_west.wait_recv()
    near, norm = process(2, sums)

    @pl.when(w == 1)
    def _():
        take(outer)

    near = jnp.sum(near, axis=0, keepdims=True)
    norm = jnp.sum(norm, axis=0, keepdims=True)
    guess = jnp.where(norm > 0.0, near / jnp.where(norm > 0.0, norm, 1.0), 0.0)

    def carried(group, k, _):
        for l in group:
            c = (-alive(l, k)) * (cf[l, k] + left_t(mt[l, k], cpack[l]))
            high, low = split(c)
            ck[l, k, 0:face] = high
            ck[l, k, face:2 * face] = low
        return 0

    def correct_one(group, k, acc):
        odd, square = acc
        for l in group:
            lower = lf[l, k, 0:face]
            e = prod[l, k] + left_t(jnp.concatenate([lower, lower], axis=0), ck[l, k])
            prod[l, k] = e
            x = xv[l, k].astype(F32).reshape(block, cols)
            e = e - guess * x
            odd = odd + fold(x * e)
            square = square + fold(e * e)
        return odd, square

    def correct(group, acc):
        @pl.when(w > 1)
        def _():
            take(group)

        lax.fori_loop(0, seg, functools.partial(carried, group), 0, unroll=4)
        once = max(1, 4 // len(group))
        return lax.fori_loop(0, seg, functools.partial(correct_one, group), acc, unroll=once)

    sums = correct(inner, (nothing, nothing))
    sums = correct(outer[:1], sums)
    odd, square = correct(outer[1:], sums)
    odd = jnp.sum(odd, axis=0, keepdims=True)
    square = jnp.sum(square, axis=0, keepdims=True)

    last = walls - 1
    stat1[...] = jnp.concatenate(
        [guess, norm, odd, square, jnp.zeros((4, cols), F32)], axis=0
    )

    def to_last(i):
        return remote(stat1, all1.at[i], s1_send.at[0], s1_recv.at[i], {"wall": last})

    def to_peer(step):
        return remote(
            stat2, all2.at[s], s2_send.at[step], s2_recv.at[step],
            {"surf": lax.rem(s + step, surfs)},
        )

    def to_wall(i):
        return remote(final, final_in, s3_send.at[i], s3_recv.at[0], {"wall": i})

    @pl.when(w < last)
    def _():
        to_last(w).start()
        to_wall(0).wait_recv()
        coefs[...] = final_in[...]
        to_last(w).wait_send()

    @pl.when(w == last)
    def _():
        for i in range(last):
            to_last(i).wait_recv()
        all1[last] = stat1[...]
        common, total, odd, square, _ = merge(all1, walls)
        block_of = jnp.concatenate(
            [common, total, odd, square, jnp.zeros((4, cols), F32)], axis=0
        )
        stat2[...] = block_of
        all2[s] = block_of
        peers = [to_peer(step) for step in range(1, surfs)]
        for copy in peers:
            copy.start()
        for copy in peers:
            copy.wait_recv()
        _, total, _, square, cross = merge(all2, surfs)
        projection = cross / total
        entries = lines * seg * block * walls * surfs
        spread = jnp.sqrt(square / entries + 1e-06)
        result = jnp.concatenate([projection, spread], axis=0)
        final[...] = result
        for i in range(last):
            to_wall(i).start()
        coefs[...] = result
        for copy in peers:
            copy.wait_send()
        for i in range(last):
            to_wall(i).wait_send()

    to_east.wait_send()
    to_west.wait_send()

    @pl.when(w < walls - 1)
    def _():
        for copy in to_above:
            copy.wait_send()
        for copy in chain:
            copy.wait_send()

    @pl.when(w > 0)
    def _():
        for copy in to_below:
            copy.wait_send()


def finish(masked, eliminated, stats, basis, coefs):
    l = pl.program_id(0)
    coefs[...] = stats[...]
    projection = stats[0:1]
    scale = 1.0 / stats[1:2]
    for k in range(basis.shape[1]):
        x = masked[l, k].astype(F32).reshape(basis.shape[2:])
        basis[0, k] = ((eliminated[l, k] - projection * x) * scale).astype(BF16)


def per_device(walls, surfs, vector, lengths, north_of, diagonal, lifting, inverse_rows):
    lines, seg, block, cols = vector.shape
    face = inverse_rows.shape[2]
    sizes = (lines, seg, block, face, cols, walls, surfs)
    stacked = lifting.reshape(lines, seg, lifting.shape[2] * face, block)
    smem = pl.BlockSpec(memory_space=pltpu.SMEM)
    vmem = pl.BlockSpec(memory_space=pltpu.VMEM)
    hbm = pl.BlockSpec(memory_space=pltpu.HBM)
    dma = pltpu.SemaphoreType.DMA
    cubes = (lines, seg, block // NODE1D**3, NODE1D**3, cols)
    slab = (seg, block // NODE1D**3, NODE1D**2, cols)
    masked, eliminated, stats = pl.pallas_call(
        functools.partial(kernel, sizes),
        out_shape=(
            pltpu.VMEM(cubes, BF16),
            pltpu.VMEM(vector.shape, F32),
            pltpu.VMEM((2, cols), F32),
        ),
        in_specs=[smem, smem, hbm, hbm, hbm, hbm],
        out_specs=(vmem, vmem, vmem),
        scratch_shapes=[
            pltpu.VMEM(diagonal.shape, BF16),
            pltpu.VMEM(stacked.shape, BF16),
            pltpu.VMEM(inverse_rows.shape, BF16),
            pltpu.VMEM((4, cols // 128, block, 128), F32),
            pltpu.VMEM((lines, seg + 1, face, cols), BF16),
            pltpu.VMEM((lines, seg + 1, face, cols), BF16),
            pltpu.VMEM((lines, seg, face, cols), BF16),
            pltpu.VMEM((lines, seg, face, cols), BF16),
            pltpu.VMEM((lines, face, cols), BF16),
            pltpu.VMEM((lines, face, cols), BF16),
            pltpu.VMEM(slab, BF16),
            pltpu.VMEM(slab, BF16),
            pltpu.VMEM((lines, seg, 3 * face, face), BF16),
            pltpu.VMEM((lines, seg + 1, 3 * face, face), BF16),
            pltpu.VMEM((lines, seg, face, cols), F32),
            pltpu.VMEM((lines, seg, face, cols), F32),
            pltpu.VMEM((lines, face, cols), F32),
            pltpu.VMEM((lines, seg, 2 * face, cols), BF16),
            pltpu.VMEM((lines, face, cols), F32),
            pltpu.VMEM((lines, 3 * face, cols), BF16),
            pltpu.VMEM((lines, face, cols), F32),
            pltpu.VMEM((8, cols), F32),
            pltpu.VMEM((walls, 8, cols), F32),
            pltpu.VMEM((8, cols), F32),
            pltpu.VMEM((surfs, 8, cols), F32),
            pltpu.VMEM((2, cols), F32),
            pltpu.VMEM((2, cols), F32),
            dma((3, 3)),
            dma((8,)),
            dma((8,)),
            dma((lines,)),
            dma((lines,)),
            dma((1,)),
            dma((walls,)),
            dma((surfs,)),
            dma((surfs,)),
            dma((walls,)),
            dma((1,)),
        ],
        compiler_params=pltpu.CompilerParams(
            collective_id=0, has_side_effects=True, vmem_limit_bytes=56 * 1024 * 1024
        ),
    )(lengths, north_of, vector.reshape(cubes), diagonal, stacked, inverse_rows)
    return pl.pallas_call(
        finish,
        grid=(lines,),
        out_shape=(
            jax.ShapeDtypeStruct(vector.shape, BF16),
            jax.ShapeDtypeStruct((2, cols), F32),
        ),
        in_specs=[vmem, vmem, vmem],
        out_specs=(
            pl.BlockSpec((1, seg, block, cols), lambda l: (l, 0, 0, 0)),
            pl.BlockSpec((2, cols), lambda l: (0, 0)),
        ),
        compiler_params=pltpu.CompilerParams(vmem_limit_bytes=16 * 1024 * 1024),
    )(masked, eliminated, stats)


def solution(mesh):
    in_specs = (
        P("surf", "wall", None, None),
        P("surf"),
        P("surf", None),
        P("surf", "wall", None, None),
        P("surf", "wall", None, None, None),
        P("surf", "wall", None, None),
    )
    out_specs = (P("surf", "wall", None, None), P())
    return jax.shard_map(
        functools.partial(per_device, mesh.shape["wall"], mesh.shape["surf"]),
        mesh=mesh, in_specs=in_specs, out_specs=out_specs, check_vma=False,
    )
```

```python
import functools

import jax
import jax.numpy as jnp
from jax import lax
from jax.experimental import pallas as pl
from jax.experimental.pallas import tpu as pltpu
from jax.sharding import PartitionSpec as P

NODE1D = 4
F32 = jnp.float32
BF16 = jnp.bfloat16
MESH = pl.DeviceIdType.MESH


def times(a, b):
    return lax.dot_general(a, b, (((1,), (0,)), ((), ())), preferred_element_type=F32)


def left_t(a, b):
    return lax.dot_general(a, b, (((0,), (0,)), ((), ())), preferred_element_type=F32)


def right_t(a, b):
    return lax.dot_general(a, b, (((1,), (1,)), ((), ())), preferred_element_type=F32)


def split(x):
    high = x.astype(BF16)
    return high, (x - high.astype(F32)).astype(BF16)


def pack(x):
    high, low = split(x)
    return jnp.concatenate([high, high, low], axis=0)


def stack(x):
    high, low = split(x)
    return jnp.concatenate([high, low, high], axis=0)


def merge(gathered, count):
    p = [gathered[i, 0:1] for i in range(count)]
    s = [gathered[i, 1:2] for i in range(count)]
    o = [gathered[i, 2:3] for i in range(count)]
    r = [gathered[i, 3:4] for i in range(count)]
    total = sum(s[1:], s[0])
    cross = sum((o[i] + p[i] * s[i] for i in range(1, count)), o[0] + p[0] * s[0])
    safe = jnp.where(total > 0.0, total, 1.0)
    common = jnp.where(total > 0.0, cross / safe, 0.0)
    odd = jnp.zeros_like(total)
    square = jnp.zeros_like(total)
    for i in range(count):
        shift = p[i] - common
        odd = odd + (o[i] + shift * s[i])
        square = square + (r[i] + shift * (2.0 * o[i] + shift * s[i]))
    return common, total, odd, square, cross


def kernel(
    sizes, lengths, north_of, vector, diagonal, lifting, inverse, xv, prod, coefs,
    dg, lf, iv, xs, top, bottom, south, north,
    below_in, above_in, west_in, east_in, at, mt, d, cf, ce, ck, cin, cpack, cout,
    stat1, all1, stat2, all2, final, final_in,
    in_sem, halo_send, halo_recv, chain_send, chain_recv,
    s1_send, s1_recv, s2_send, s2_recv, s3_send, s3_recv,
):
    lines, seg, block, face, cols, walls, surfs = sizes
    w = lax.axis_index("wall")
    s = lax.axis_index("surf")
    plane = NODE1D * NODE1D
    cube = plane * NODE1D
    outer = [0, lines - 1]
    inner = list(range(1, lines - 1))

    groups = [inner, outer[:1], outer[1:]]
    load_x = pltpu.make_async_copy(vector, xv, in_sem.at[0, 0])
    load_iv = pltpu.make_async_copy(inverse, iv, in_sem.at[0, 1])
    load_lf, load_dg = [], []
    for n, group in enumerate(groups):
        part = slice(group[0], group[-1] + 1)
        load_lf.append(
            pltpu.make_async_copy(lifting.at[part], lf.at[part], in_sem.at[1, n])
        )
        load_dg.append(
            pltpu.make_async_copy(diagonal.at[part], dg.at[part], in_sem.at[2, n])
        )
    load_x.start()
    load_iv.start()
    for n in range(len(groups)):
        load_lf[n].start()
        load_dg[n].start()
    barrier = pltpu.get_barrier_semaphore()
    for step in range(1, walls):
        pl.semaphore_signal(
            barrier, inc=1, device_id={"wall": lax.rem(w + step, walls)}, device_id_type=MESH
        )
    for step in range(1, surfs):
        pl.semaphore_signal(
            barrier, inc=1, device_id={"surf": lax.rem(s + step, surfs)}, device_id_type=MESH
        )

    def alive(l, k):
        return jnp.where(w * seg + k < lengths[l], 1.0, 0.0).astype(F32)

    def mask_line(l):
        def one(k, _):
            x = xv[l, k].astype(F32).reshape(block, cols) * alive(l, k)
            xv[l, k] = x.astype(BF16).reshape(xv.shape[2:])
            return 0

        lax.fori_loop(0, seg, one, 0)

    load_x.wait()
    for l in outer:
        mask_line(l)
    pl.semaphore_wait(barrier, walls - 1 + surfs - 1)

    def remote(src, dst, send, recv, target):
        return pltpu.make_async_remote_copy(
            src_ref=src, dst_ref=dst, send_sem=send, recv_sem=recv,
            device_id=target, device_id_type=MESH,
        )

    to_east = remote(
        xv.at[lines - 1, :, :, cube - plane:cube], west_in, halo_send.at[0], halo_recv.at[0],
        {"surf": lax.rem(s + 1, surfs)},
    )
    to_west = remote(
        xv.at[0, :, :, 0:plane], east_in, halo_send.at[1], halo_recv.at[1],
        {"surf": lax.rem(s + surfs - 1, surfs)},
    )
    to_east.start()
    to_west.start()
    for l in inner:
        mask_line(l)

    count = block // plane

    def trace_one(l, k, i):
        x = xv[l, k].astype(F32).reshape(block, cols)
        slot = lax.rem(i, 4)
        for h in range(cols // 128):
            xs[slot, h] = x[:, h * 128:(h + 1) * 128]
        for h in range(cols // 128):
            at_h = pl.ds(h * 128, 128)
            bottom[l, k, :, at_h] = xs[slot, h, pl.ds(0, face, stride=NODE1D), :].astype(BF16)
            top[l, k + 1, :, at_h] = xs[
                slot, h, pl.ds(NODE1D - 1, face, stride=NODE1D), :
            ].astype(BF16)
        y = x.reshape(count, plane, cols)
        south[l, k] = y[:, 0:NODE1D].reshape(face, cols).astype(BF16)
        north[l, k] = y[:, plane - NODE1D:plane].reshape(face, cols).astype(BF16)

    def trace_ends(group, i, _):
        for l in group:
            trace_one(l, i * (seg - 1), 2 * i + group.index(l))
        return 0

    def trace_rest(i, _):
        trace_one(i // (seg - 2), 1 + i % (seg - 2), i)
        return 0


    up = {"wall": lax.rem(w + 1, walls)}
    down = {"wall": lax.rem(w + walls - 1, walls)}
    to_above, to_below = [], []
    for n, group in enumerate(groups):
        part = slice(group[0], group[-1] + 1)
        to_above.append(remote(
            top.at[part, seg], below_in.at[part], halo_send.at[2 + n], halo_recv.at[2 + n], up
        ))
        m = 2 + len(groups) + n
        to_below.append(remote(
            bottom.at[part, 0], above_in.at[part], halo_send.at[m], halo_recv.at[m], down
        ))

    def greet(parts):
        @pl.when(w < walls - 1)
        def _():
            for n in parts:
                to_above[n].start()

        @pl.when(w > 0)
        def _():
            for n in parts:
                to_below[n].start()

    lax.fori_loop(0, 2, functools.partial(trace_ends, inner), 0, unroll=2)
    greet([0])
    lax.fori_loop(0, 2, functools.partial(trace_ends, outer), 0, unroll=2)
    greet([1, 2])
    lax.fori_loop(0, lines * (seg - 2), trace_rest, 0, unroll=4)
    row = lax.broadcasted_iota(jnp.int32, (face, face), 0)
    column = lax.broadcasted_iota(jnp.int32, (face, face), 1)
    eye = jnp.where(row == column, 1.0, 0.0).astype(F32)

    def three(left, right):
        lh, ll = left[0:face], left[face:2 * face]
        rh, rl = right[0:face], right[face:2 * face]
        return times(lh, rh) + (times(ll, rh) + times(lh, rl))

    def map_one(group, k, _):
        for l in group:
            a = (-alive(l, k)) * right_t(lf[l, k, 0:face], iv[l, k])
            at[l, k] = stack(a)
        return 0

    load_iv.wait()
    for copy in load_lf:
        copy.wait()
    lax.fori_loop(0, seg, functools.partial(map_one, inner + outer), 0, unroll=4)

    @pl.when(w == 0)
    def _():
        mt[...] = jnp.zeros_like(mt)

    @pl.when(w > 0)
    def _():
        for l in range(lines):
            mt[l, 0] = stack(eye)
            mt[l, 1] = at[l, 0]
        for k in range(1, seg):
            for l in range(lines):
                mt[l, k + 1] = stack(three(mt[l, k], at[l, k]))

    south_of = []
    for l in range(lines):
        line = jnp.int32(0)
        for j in range(lines):
            line = jnp.where(north_of[0, j] == l, j, line)
        south_of.append(line)

    def fold(x):
        return jnp.sum(x.reshape(block // 8, 8, cols), axis=0)

    def local_step(group, k, acc):
        near, norm = acc
        for l in group:
            x = xv[l, k].reshape(block, cols)
            if l > 0:
                west = xv[l - 1, k, :, cube - plane:cube]
            else:
                west = west_in[k]
            if l < lines - 1:
                east = xv[l + 1, k, :, 0:plane]
            else:
                east = east_in[k]
            sides = [
                top[l, k], bottom[l, k + 1], west.reshape(face, cols), east.reshape(face, cols),
                north[south_of[l], k], south[north_of[0, l], k],
            ]
            p = times(dg[l, k], x) + left_t(lf[l, k], jnp.concatenate(sides, axis=0))
            p = alive(l, k) * p
            prod[l, k] = p
            wide = x.astype(F32)
            near = near + fold(wide * p)
            norm = norm + fold(wide * wide)
        return near, norm

    def inverse_step(group, k, _):
        for l in group:
            high, low = split(prod[l, k])
            d[l, k] = times(iv[l, k], high) + times(iv[l, k], low)
        return 0

    nothing = jnp.zeros((8, cols), F32)

    def meet(n):
        group = groups[n]

        @pl.when(w > 0)
        def _():
            to_above[n].wait_recv()
            for l in group:
                top[l, 0] = below_in[l]

        @pl.when(w == 0)
        def _():
            for l in group:
                top[l, 0] = jnp.zeros((face, cols), BF16)

        @pl.when(w < walls - 1)
        def _():
            to_below[n].wait_recv()
            for l in group:
                bottom[l, seg] = above_in[l]

        @pl.when(w == walls - 1)
        def _():
            for l in group:
                bottom[l, seg] = jnp.zeros((face, cols), BF16)

    chain = [
        remote(cout.at[l], cin.at[l], chain_send.at[l], chain_recv.at[l], up)
        for l in range(lines)
    ]

    def begin(group):
        @pl.when(w == 0)
        def _():
            for l in group:
                cout[l] = ce[l]
                chain[l].start()

    def take(group):
        for l in group:
            chain[l].wait_recv()
            cpack[l] = pack(cin[l])

            @pl.when(w < walls - 1)
            def _():
                cout[l] = ce[l] + left_t(mt[l, seg], cpack[l])
                chain[l].start()

    def process(n, acc):
        group = groups[n]
        load_dg[n].wait()
        once = 4
        meet(n)
        acc = lax.fori_loop(0, seg, functools.partial(local_step, group), acc, unroll=once)
        lax.fori_loop(0, seg, functools.partial(inverse_step, group), 0, unroll=4)
        for l in group:
            cf[l, 0] = jnp.zeros((face, cols), F32)
            cf[l, 1] = d[l, 0]
        for k in range(1, seg):
            for l in group:
                c = d[l, k] + left_t(at[l, k], pack(cf[l, k]))
                if k < seg - 1:
                    cf[l, k + 1] = c
                else:
                    ce[l] = c
        begin(group)
        return acc

    @pl.when(w == 0)
    def _():
        cpack[...] = jnp.zeros_like(cpack)

    sums = process(0, (nothing, nothing))
    to_east.wait_recv()
    sums = process(1, sums)

    @pl.when(w == 1)
    def _():
        take(inner)

    to_west.wait_recv()
    near, norm = process(2, sums)

    @pl.when(w == 1)
    def _():
        take(outer)

    near = jnp.sum(near, axis=0, keepdims=True)
    norm = jnp.sum(norm, axis=0, keepdims=True)
    guess = jnp.where(norm > 0.0, near / jnp.where(norm > 0.0, norm, 1.0), 0.0)

    def carried(group, k, _):
        for l in group:
            c = (-alive(l, k)) * (cf[l, k] + left_t(mt[l, k], cpack[l]))
            high, low = split(c)
            ck[l, k, 0:face] = high
            ck[l, k, face:2 * face] = low
        return 0

    def correct_one(group, k, acc):
        odd, square = acc
        for l in group:
            lower = lf[l, k, 0:face]
            e = prod[l, k] + left_t(jnp.concatenate([lower, lower], axis=0), ck[l, k])
            prod[l, k] = e
            x = xv[l, k].astype(F32).reshape(block, cols)
            e = e - guess * x
            odd = odd + fold(x * e)
            square = square + fold(e * e)
        return odd, square

    def correct(group, acc):
        @pl.when(w > 1)
        def _():
            take(group)

        lax.fori_loop(0, seg, functools.partial(carried, group), 0, unroll=4)
        once = 4
        return lax.fori_loop(0, seg, functools.partial(correct_one, group), acc, unroll=once)

    sums = correct(inner, (nothing, nothing))
    sums = correct(outer[:1], sums)
    odd, square = correct(outer[1:], sums)
    odd = jnp.sum(odd, axis=0, keepdims=True)
    square = jnp.sum(square, axis=0, keepdims=True)

    last = walls - 1
    stat1[...] = jnp.concatenate(
        [guess, norm, odd, square, jnp.zeros((4, cols), F32)], axis=0
    )

    def to_last(i):
        return remote(stat1, all1.at[i], s1_send.at[0], s1_recv.at[i], {"wall": last})

    def to_peer(step):
        return remote(
            stat2, all2.at[s], s2_send.at[step], s2_recv.at[step],
            {"surf": lax.rem(s + step, surfs)},
        )

    def to_wall(i):
        return remote(final, final_in, s3_send.at[i], s3_recv.at[0], {"wall": i})

    @pl.when(w < last)
    def _():
        to_last(w).start()
        to_wall(0).wait_recv()
        coefs[...] = final_in[...]
        to_last(w).wait_send()

    @pl.when(w == last)
    def _():
        for i in range(last):
            to_last(i).wait_recv()
        all1[last] = stat1[...]
        common, total, odd, square, _ = merge(all1, walls)
        block_of = jnp.concatenate(
            [common, total, odd, square, jnp.zeros((4, cols), F32)], axis=0
        )
        stat2[...] = block_of
        all2[s] = block_of
        peers = [to_peer(step) for step in range(1, surfs)]
        for copy in peers:
            copy.start()
        for copy in peers:
            copy.wait_recv()
        _, total, _, square, cross = merge(all2, surfs)
        projection = cross / total
        entries = lines * seg * block * walls * surfs
        spread = jnp.sqrt(square / entries + 1e-06)
        result = jnp.concatenate([projection, spread], axis=0)
        final[...] = result
        for i in range(last):
            to_wall(i).start()
        coefs[...] = result
        for copy in peers:
            copy.wait_send()
        for i in range(last):
            to_wall(i).wait_send()

    to_east.wait_send()
    to_west.wait_send()

    @pl.when(w < walls - 1)
    def _():
        for copy in to_above:
            copy.wait_send()
        for copy in chain:
            copy.wait_send()

    @pl.when(w > 0)
    def _():
        for copy in to_below:
            copy.wait_send()


def finish(masked, eliminated, stats, basis, coefs):
    l = pl.program_id(0)
    coefs[...] = stats[...]
    projection = stats[0:1]
    scale = 1.0 / stats[1:2]
    pair = basis.shape[0]
    for h in range(pair):
        for k in range(basis.shape[1]):
            x = masked[pair * l + h, k].astype(F32).reshape(basis.shape[2:])
            basis[h, k] = ((eliminated[pair * l + h, k] - projection * x) * scale).astype(BF16)


def per_device(walls, surfs, vector, lengths, north_of, diagonal, lifting, inverse_rows):
    lines, seg, block, cols = vector.shape
    face = inverse_rows.shape[2]
    sizes = (lines, seg, block, face, cols, walls, surfs)
    stacked = lifting.reshape(lines, seg, lifting.shape[2] * face, block)
    smem = pl.BlockSpec(memory_space=pltpu.SMEM)
    vmem = pl.BlockSpec(memory_space=pltpu.VMEM)
    hbm = pl.BlockSpec(memory_space=pltpu.HBM)
    dma = pltpu.SemaphoreType.DMA
    cubes = (lines, seg, block // NODE1D**3, NODE1D**3, cols)
    slab = (seg, block // NODE1D**3, NODE1D**2, cols)
    masked, eliminated, stats = pl.pallas_call(
        functools.partial(kernel, sizes),
        out_shape=(
            pltpu.VMEM(cubes, BF16),
            pltpu.VMEM(vector.shape, F32),
            pltpu.VMEM((2, cols), F32),
        ),
        in_specs=[smem, smem, hbm, hbm, hbm, hbm],
        out_specs=(vmem, vmem, vmem),
        scratch_shapes=[
            pltpu.VMEM(diagonal.shape, BF16),
            pltpu.VMEM(stacked.shape, BF16),
            pltpu.VMEM(inverse_rows.shape, BF16),
            pltpu.VMEM((4, cols // 128, block, 128), F32),
            pltpu.VMEM((lines, seg + 1, face, cols), BF16),
            pltpu.VMEM((lines, seg + 1, face, cols), BF16),
            pltpu.VMEM((lines, seg, face, cols), BF16),
            pltpu.VMEM((lines, seg, face, cols), BF16),
            pltpu.VMEM((lines, face, cols), BF16),
            pltpu.VMEM((lines, face, cols), BF16),
            pltpu.VMEM(slab, BF16),
            pltpu.VMEM(slab, BF16),
            pltpu.VMEM((lines, seg, 3 * face, face), BF16),
            pltpu.VMEM((lines, seg + 1, 3 * face, face), BF16),
            pltpu.VMEM((lines, seg, face, cols), F32),
            pltpu.VMEM((lines, seg, face, cols), F32),
            pltpu.VMEM((lines, face, cols), F32),
            pltpu.VMEM((lines, seg, 2 * face, cols), BF16),
            pltpu.VMEM((lines, face, cols), F32),
            pltpu.VMEM((lines, 3 * face, cols), BF16),
            pltpu.VMEM((lines, face, cols), F32),
            pltpu.VMEM((8, cols), F32),
            pltpu.VMEM((walls, 8, cols), F32),
            pltpu.VMEM((8, cols), F32),
            pltpu.VMEM((surfs, 8, cols), F32),
            pltpu.VMEM((2, cols), F32),
            pltpu.VMEM((2, cols), F32),
            dma((3, 3)),
            dma((8,)),
            dma((8,)),
            dma((lines,)),
            dma((lines,)),
            dma((1,)),
            dma((walls,)),
            dma((surfs,)),
            dma((surfs,)),
            dma((walls,)),
            dma((1,)),
        ],
        compiler_params=pltpu.CompilerParams(
            collective_id=0, has_side_effects=True, vmem_limit_bytes=56 * 1024 * 1024
        ),
    )(lengths, north_of, vector.reshape(cubes), diagonal, stacked, inverse_rows)
    pair = 2 if lines % 2 == 0 else 1
    return pl.pallas_call(
        finish,
        grid=(lines // pair,),
        out_shape=(
            jax.ShapeDtypeStruct(vector.shape, BF16),
            jax.ShapeDtypeStruct((2, cols), F32),
        ),
        in_specs=[vmem, vmem, vmem],
        out_specs=(
            pl.BlockSpec((pair, seg, block, cols), lambda l: (l, 0, 0, 0)),
            pl.BlockSpec((2, cols), lambda l: (0, 0)),
        ),
        compiler_params=pltpu.CompilerParams(vmem_limit_bytes=16 * 1024 * 1024),
    )(masked, eliminated, stats)


def solution(mesh):
    in_specs = (
        P("surf", "wall", None, None),
        P("surf"),
        P("surf", None),
        P("surf", "wall", None, None),
        P("surf", "wall", None, None, None),
        P("surf", "wall", None, None),
    )
    out_specs = (P("surf", "wall", None, None), P())
    return jax.shard_map(
        functools.partial(per_device, mesh.shape["wall"], mesh.shape["surf"]),
        mesh=mesh, in_specs=in_specs, out_specs=out_specs, check_vma=False,
    )
```

```python
import functools

import jax
import jax.numpy as jnp
from jax import lax
from jax.experimental import pallas as pl
from jax.experimental.pallas import tpu as pltpu
from jax.sharding import PartitionSpec as P

NODE1D = 4
F32 = jnp.float32
BF16 = jnp.bfloat16
MESH = pl.DeviceIdType.MESH


def times(a, b):
    return lax.dot_general(a, b, (((1,), (0,)), ((), ())), preferred_element_type=F32)


def left_t(a, b):
    return lax.dot_general(a, b, (((0,), (0,)), ((), ())), preferred_element_type=F32)


def right_t(a, b):
    return lax.dot_general(a, b, (((1,), (1,)), ((), ())), preferred_element_type=F32)


def split(x):
    high = x.astype(BF16)
    return high, (x - high.astype(F32)).astype(BF16)


def pack(x):
    high, low = split(x)
    return jnp.concatenate([high, high, low], axis=0)


def stack(x):
    high, low = split(x)
    return jnp.concatenate([high, low, high], axis=0)


def merge(gathered, count):
    p = [gathered[i, 0:1] for i in range(count)]
    s = [gathered[i, 1:2] for i in range(count)]
    o = [gathered[i, 2:3] for i in range(count)]
    r = [gathered[i, 3:4] for i in range(count)]
    total = sum(s[1:], s[0])
    cross = sum((o[i] + p[i] * s[i] for i in range(1, count)), o[0] + p[0] * s[0])
    safe = jnp.where(total > 0.0, total, 1.0)
    common = jnp.where(total > 0.0, cross / safe, 0.0)
    odd = jnp.zeros_like(total)
    square = jnp.zeros_like(total)
    for i in range(count):
        shift = p[i] - common
        odd = odd + (o[i] + shift * s[i])
        square = square + (r[i] + shift * (2.0 * o[i] + shift * s[i]))
    return common, total, odd, square, cross


def kernel(
    sizes, lengths, north_of, vector, diagonal, lifting, inverse, xv, prod, coefs,
    dg, lf, iv, xs, top, bottom, south, north,
    below_in, above_in, west_in, east_in, at, mt, d, cf, ce, ck, cin, cpack, cout,
    stat1, all1, stat2, all2, final, final_in,
    in_sem, halo_send, halo_recv, chain_send, chain_recv,
    s1_send, s1_recv, s2_send, s2_recv, s3_send, s3_recv,
):
    lines, seg, block, face, cols, walls, surfs = sizes
    w = lax.axis_index("wall")
    s = lax.axis_index("surf")
    plane = NODE1D * NODE1D
    cube = plane * NODE1D
    outer = [0, lines - 1]
    inner = list(range(1, lines - 1))

    groups = [inner, outer[:1], outer[1:]]
    load_x = pltpu.make_async_copy(vector, xv, in_sem.at[0, 0])
    load_iv = pltpu.make_async_copy(inverse, iv, in_sem.at[0, 1])
    load_lf, load_dg = [], []
    for n, group in enumerate(groups):
        part = slice(group[0], group[-1] + 1)
        load_lf.append(
            pltpu.make_async_copy(lifting.at[part], lf.at[part], in_sem.at[1, n])
        )
        load_dg.append(
            pltpu.make_async_copy(diagonal.at[part], dg.at[part], in_sem.at[2, n])
        )
    load_x.start()
    load_iv.start()
    for copy in load_lf + load_dg:
        copy.start()
    barrier = pltpu.get_barrier_semaphore()
    for step in range(1, walls):
        pl.semaphore_signal(
            barrier, inc=1, device_id={"wall": lax.rem(w + step, walls)}, device_id_type=MESH
        )
    for step in range(1, surfs):
        pl.semaphore_signal(
            barrier, inc=1, device_id={"surf": lax.rem(s + step, surfs)}, device_id_type=MESH
        )

    def alive(l, k):
        return jnp.where(w * seg + k < lengths[l], 1.0, 0.0).astype(F32)

    def mask_line(l):
        def one(k, _):
            x = xv[l, k].astype(F32).reshape(block, cols) * alive(l, k)
            xv[l, k] = x.astype(BF16).reshape(xv.shape[2:])
            return 0

        lax.fori_loop(0, seg, one, 0, unroll=seg)

    load_x.wait()
    for l in outer:
        mask_line(l)
    pl.semaphore_wait(barrier, walls - 1 + surfs - 1)

    def remote(src, dst, send, recv, target):
        return pltpu.make_async_remote_copy(
            src_ref=src, dst_ref=dst, send_sem=send, recv_sem=recv,
            device_id=target, device_id_type=MESH,
        )

    to_east = remote(
        xv.at[lines - 1, :, :, cube - plane:cube], west_in, halo_send.at[0], halo_recv.at[0],
        {"surf": lax.rem(s + 1, surfs)},
    )
    to_west = remote(
        xv.at[0, :, :, 0:plane], east_in, halo_send.at[1], halo_recv.at[1],
        {"surf": lax.rem(s + surfs - 1, surfs)},
    )
    to_east.start()
    to_west.start()
    for l in inner:
        mask_line(l)

    count = block // plane

    def trace_one(l, k, i):
        x = xv[l, k].astype(F32).reshape(block, cols)
        slot = lax.rem(i, 4)
        for h in range(cols // 128):
            xs[slot, h] = x[:, h * 128:(h + 1) * 128]
        for h in range(cols // 128):
            at_h = pl.ds(h * 128, 128)
            bottom[l, k, :, at_h] = xs[slot, h, pl.ds(0, face, stride=NODE1D), :].astype(BF16)
            top[l, k + 1, :, at_h] = xs[
                slot, h, pl.ds(NODE1D - 1, face, stride=NODE1D), :
            ].astype(BF16)
        y = x.reshape(count, plane, cols)
        south[l, k] = y[:, 0:NODE1D].reshape(face, cols).astype(BF16)
        north[l, k] = y[:, plane - NODE1D:plane].reshape(face, cols).astype(BF16)

    def trace_ends(group, i, _):
        for l in group:
            trace_one(l, i * (seg - 1), 2 * i + group.index(l))
        return 0

    def trace_rest(i, _):
        trace_one(i // (seg - 2), 1 + i % (seg - 2), i)
        return 0


    up = {"wall": lax.rem(w + 1, walls)}
    down = {"wall": lax.rem(w + walls - 1, walls)}
    to_above, to_below = [], []
    for n, group in enumerate(groups):
        part = slice(group[0], group[-1] + 1)
        to_above.append(remote(
            top.at[part, seg], below_in.at[part], halo_send.at[2 + n], halo_recv.at[2 + n], up
        ))
        m = 2 + len(groups) + n
        to_below.append(remote(
            bottom.at[part, 0], above_in.at[part], halo_send.at[m], halo_recv.at[m], down
        ))

    def greet(parts):
        @pl.when(w < walls - 1)
        def _():
            for n in parts:
                to_above[n].start()

        @pl.when(w > 0)
        def _():
            for n in parts:
                to_below[n].start()

    lax.fori_loop(0, 2, functools.partial(trace_ends, inner), 0, unroll=2)
    greet([0])
    lax.fori_loop(0, 2, functools.partial(trace_ends, outer), 0, unroll=2)
    greet([1, 2])
    lax.fori_loop(0, lines * (seg - 2), trace_rest, 0, unroll=4)
    row = lax.broadcasted_iota(jnp.int32, (face, face), 0)
    column = lax.broadcasted_iota(jnp.int32, (face, face), 1)
    eye = jnp.where(row == column, 1.0, 0.0).astype(F32)

    def three(left, right):
        lh, ll = left[0:face], left[face:2 * face]
        rh, rl = right[0:face], right[face:2 * face]
        return times(lh, rh) + (times(ll, rh) + times(lh, rl))

    def map_one(group, k, _):
        for l in group:
            a = (-alive(l, k)) * right_t(lf[l, k, 0:face], iv[l, k])
            at[l, k] = stack(a)
        return 0

    load_iv.wait()
    for copy in load_lf:
        copy.wait()
    lax.fori_loop(0, seg, functools.partial(map_one, inner + outer), 0, unroll=4)

    @pl.when(w == 0)
    def _():
        mt[...] = jnp.zeros_like(mt)

    @pl.when(w > 0)
    def _():
        for l in range(lines):
            mt[l, 0] = stack(eye)
            mt[l, 1] = at[l, 0]
        for k in range(1, seg):
            for l in range(lines):
                mt[l, k + 1] = stack(three(mt[l, k], at[l, k]))

    south_of = []
    for l in range(lines):
        line = jnp.int32(0)
        for j in range(lines):
            line = jnp.where(north_of[0, j] == l, j, line)
        south_of.append(line)

    def fold(x):
        return jnp.sum(x.reshape(block // 8, 8, cols), axis=0)

    def local_step(group, k, acc):
        near, norm = acc
        for l in group:
            x = xv[l, k].reshape(block, cols)
            if l > 0:
                west = xv[l - 1, k, :, cube - plane:cube]
            else:
                west = west_in[k]
            if l < lines - 1:
                east = xv[l + 1, k, :, 0:plane]
            else:
                east = east_in[k]
            sides = [
                top[l, k], bottom[l, k + 1], west.reshape(face, cols), east.reshape(face, cols),
                north[south_of[l], k], south[north_of[0, l], k],
            ]
            p = times(dg[l, k], x) + left_t(lf[l, k], jnp.concatenate(sides, axis=0))
            p = alive(l, k) * p
            prod[l, k] = p
            wide = x.astype(F32)
            near = near + fold(wide * p)
            norm = norm + fold(wide * wide)
        return near, norm

    def inverse_step(group, k, _):
        for l in group:
            high, low = split(prod[l, k])
            d[l, k] = times(iv[l, k], high) + times(iv[l, k], low)
        return 0

    nothing = jnp.zeros((8, cols), F32)

    def meet(n):
        group = groups[n]

        @pl.when(w > 0)
        def _():
            to_above[n].wait_recv()
            for l in group:
                top[l, 0] = below_in[l]

        @pl.when(w == 0)
        def _():
            for l in group:
                top[l, 0] = jnp.zeros((face, cols), BF16)

        @pl.when(w < walls - 1)
        def _():
            to_below[n].wait_recv()
            for l in group:
                bottom[l, seg] = above_in[l]

        @pl.when(w == walls - 1)
        def _():
            for l in group:
                bottom[l, seg] = jnp.zeros((face, cols), BF16)

    chain = [
        remote(cout.at[l], cin.at[l], chain_send.at[l], chain_recv.at[l], up)
        for l in range(lines)
    ]

    def begin(group):
        @pl.when(w == 0)
        def _():
            for l in group:
                cout[l] = ce[l]
                chain[l].start()

    def take(group):
        for l in group:
            chain[l].wait_recv()
            cpack[l] = pack(cin[l])

            @pl.when(w < walls - 1)
            def _():
                cout[l] = ce[l] + left_t(mt[l, seg], cpack[l])
                chain[l].start()

    def process(n, acc):
        group = groups[n]
        load_dg[n].wait()
        once = 4
        meet(n)
        acc = lax.fori_loop(0, seg, functools.partial(local_step, group), acc, unroll=once)
        lax.fori_loop(0, seg, functools.partial(inverse_step, group), 0, unroll=seg)
        for l in group:
            cf[l, 0] = jnp.zeros((face, cols), F32)
            cf[l, 1] = d[l, 0]
        for k in range(1, seg):
            for l in group:
                c = d[l, k] + left_t(at[l, k], pack(cf[l, k]))
                if k < seg - 1:
                    cf[l, k + 1] = c
                else:
                    ce[l] = c
        begin(group)
        return acc

    @pl.when(w == 0)
    def _():
        cpack[...] = jnp.zeros_like(cpack)

    sums = process(0, (nothing, nothing))
    to_east.wait_recv()
    sums = process(1, sums)

    @pl.when(w == 1)
    def _():
        take(inner)

    to_west.wait_recv()
    near, norm = process(2, sums)

    @pl.when(w == 1)
    def _():
        take(outer)

    near = jnp.sum(near, axis=0, keepdims=True)
    norm = jnp.sum(norm, axis=0, keepdims=True)
    guess = jnp.where(norm > 0.0, near / jnp.where(norm > 0.0, norm, 1.0), 0.0)

    def carried(group, k, _):
        for l in group:
            c = (-alive(l, k)) * (cf[l, k] + left_t(mt[l, k], cpack[l]))
            high, low = split(c)
            ck[l, k, 0:face] = high
            ck[l, k, face:2 * face] = low
        return 0

    def correct_one(group, k, acc):
        odd, square = acc
        for l in group:
            lower = lf[l, k, 0:face]
            e = prod[l, k] + left_t(jnp.concatenate([lower, lower], axis=0), ck[l, k])
            prod[l, k] = e
            x = xv[l, k].astype(F32).reshape(block, cols)
            e = e - guess * x
            odd = odd + fold(x * e)
            square = square + fold(e * e)
        return odd, square

    def correct(group, acc):
        @pl.when(w > 1)
        def _():
            take(group)

        lax.fori_loop(0, seg, functools.partial(carried, group), 0, unroll=4)
        once = 4
        return lax.fori_loop(0, seg, functools.partial(correct_one, group), acc, unroll=once)

    sums = correct(inner, (nothing, nothing))
    sums = correct(outer[:1], sums)
    odd, square = correct(outer[1:], sums)
    odd = jnp.sum(odd, axis=0, keepdims=True)
    square = jnp.sum(square, axis=0, keepdims=True)

    last = walls - 1
    stat1[...] = jnp.concatenate(
        [guess, norm, odd, square], axis=0
    )

    def to_last(i):
        return remote(stat1, all1.at[i], s1_send.at[0], s1_recv.at[i], {"wall": last})

    def to_peer(step):
        return remote(
            stat2, all2.at[s], s2_send.at[step], s2_recv.at[step],
            {"surf": lax.rem(s + step, surfs)},
        )

    def to_wall(i):
        return remote(final, final_in, s3_send.at[i], s3_recv.at[0], {"wall": i})

    @pl.when(w < last)
    def _():
        to_last(w).start()
        to_wall(0).wait_recv()
        coefs[...] = final_in[...]
        to_last(w).wait_send()

    @pl.when(w == last)
    def _():
        for i in range(last):
            to_last(i).wait_recv()
        all1[last] = stat1[...]
        common, total, odd, square, _ = merge(all1, walls)
        block_of = jnp.concatenate(
            [common, total, odd, square], axis=0
        )
        stat2[...] = block_of
        all2[s] = block_of
        peers = [to_peer(step) for step in range(1, surfs)]
        for copy in peers:
            copy.start()
        for copy in peers:
            copy.wait_recv()
        _, total, _, square, cross = merge(all2, surfs)
        projection = cross / total
        entries = lines * seg * block * walls * surfs
        spread = jnp.sqrt(square / entries + 1e-06)
        result = jnp.concatenate([projection, spread], axis=0)
        final[...] = result
        for i in range(last):
            to_wall(i).start()
        coefs[...] = result
        for copy in peers:
            copy.wait_send()
        for i in range(last):
            to_wall(i).wait_send()

    to_east.wait_send()
    to_west.wait_send()

    @pl.when(w < walls - 1)
    def _():
        for copy in to_above:
            copy.wait_send()
        for copy in chain:
            copy.wait_send()

    @pl.when(w > 0)
    def _():
        for copy in to_below:
            copy.wait_send()


def finish(masked, eliminated, stats, basis, coefs):
    l = pl.program_id(0)
    coefs[...] = stats[...]
    projection = stats[0:1]
    scale = 1.0 / stats[1:2]
    pair = basis.shape[0]
    for h in range(pair):
        for k in range(basis.shape[1]):
            x = masked[pair * l + h, k].astype(F32).reshape(basis.shape[2:])
            basis[h, k] = ((eliminated[pair * l + h, k] - projection * x) * scale).astype(BF16)


def per_device(walls, surfs, vector, lengths, north_of, diagonal, lifting, inverse_rows):
    lines, seg, block, cols = vector.shape
    face = inverse_rows.shape[2]
    sizes = (lines, seg, block, face, cols, walls, surfs)
    stacked = lifting.reshape(lines, seg, lifting.shape[2] * face, block)
    smem = pl.BlockSpec(memory_space=pltpu.SMEM)
    vmem = pl.BlockSpec(memory_space=pltpu.VMEM)
    hbm = pl.BlockSpec(memory_space=pltpu.HBM)
    dma = pltpu.SemaphoreType.DMA
    cubes = (lines, seg, block // NODE1D**3, NODE1D**3, cols)
    slab = (seg, block // NODE1D**3, NODE1D**2, cols)
    masked, eliminated, stats = pl.pallas_call(
        functools.partial(kernel, sizes),
        out_shape=(
            pltpu.VMEM(cubes, BF16),
            pltpu.VMEM(vector.shape, F32),
            pltpu.VMEM((2, cols), F32),
        ),
        in_specs=[smem, smem, hbm, hbm, hbm, hbm],
        out_specs=(vmem, vmem, vmem),
        scratch_shapes=[
            pltpu.VMEM(diagonal.shape, BF16),
            pltpu.VMEM(stacked.shape, BF16),
            pltpu.VMEM(inverse_rows.shape, BF16),
            pltpu.VMEM((4, cols // 128, block, 128), F32),
            pltpu.VMEM((lines, seg + 1, face, cols), BF16),
            pltpu.VMEM((lines, seg + 1, face, cols), BF16),
            pltpu.VMEM((lines, seg, face, cols), BF16),
            pltpu.VMEM((lines, seg, face, cols), BF16),
            pltpu.VMEM((lines, face, cols), BF16),
            pltpu.VMEM((lines, face, cols), BF16),
            pltpu.VMEM(slab, BF16),
            pltpu.VMEM(slab, BF16),
            pltpu.VMEM((lines, seg, 3 * face, face), BF16),
            pltpu.VMEM((lines, seg + 1, 3 * face, face), BF16),
            pltpu.VMEM((lines, seg, face, cols), F32),
            pltpu.VMEM((lines, seg, face, cols), F32),
            pltpu.VMEM((lines, face, cols), F32),
            pltpu.VMEM((lines, seg, 2 * face, cols), BF16),
            pltpu.VMEM((lines, face, cols), F32),
            pltpu.VMEM((lines, 3 * face, cols), BF16),
            pltpu.VMEM((lines, face, cols), F32),
            pltpu.VMEM((4, cols), F32),
            pltpu.VMEM((walls, 4, cols), F32),
            pltpu.VMEM((4, cols), F32),
            pltpu.VMEM((surfs, 4, cols), F32),
            pltpu.VMEM((2, cols), F32),
            pltpu.VMEM((2, cols), F32),
            dma((3, 3)),
            dma((8,)),
            dma((8,)),
            dma((lines,)),
            dma((lines,)),
            dma((1,)),
            dma((walls,)),
            dma((surfs,)),
            dma((surfs,)),
            dma((walls,)),
            dma((1,)),
        ],
        compiler_params=pltpu.CompilerParams(
            collective_id=0, has_side_effects=True, vmem_limit_bytes=56 * 1024 * 1024
        ),
    )(lengths, north_of, vector.reshape(cubes), diagonal, stacked, inverse_rows)
    pair = 2 if lines % 2 == 0 else 1
    return pl.pallas_call(
        finish,
        grid=(lines // pair,),
        out_shape=(
            jax.ShapeDtypeStruct(vector.shape, BF16),
            jax.ShapeDtypeStruct((2, cols), F32),
        ),
        in_specs=[vmem, vmem, vmem],
        out_specs=(
            pl.BlockSpec((pair, seg, block, cols), lambda l: (l, 0, 0, 0)),
            pl.BlockSpec((2, cols), lambda l: (0, 0)),
        ),
        compiler_params=pltpu.CompilerParams(vmem_limit_bytes=16 * 1024 * 1024),
    )(masked, eliminated, stats)


def solution(mesh):
    in_specs = (
        P("surf", "wall", None, None),
        P("surf"),
        P("surf", None),
        P("surf", "wall", None, None),
        P("surf", "wall", None, None, None),
        P("surf", "wall", None, None),
    )
    out_specs = (P("surf", "wall", None, None), P())
    return jax.shard_map(
        functools.partial(per_device, mesh.shape["wall"], mesh.shape["surf"]),
        mesh=mesh, in_specs=in_specs, out_specs=out_specs, check_vma=False,
    )
```

```python
import functools

import jax
import jax.numpy as jnp
from jax import lax
from jax.experimental import pallas as pl
from jax.experimental.pallas import tpu as pltpu
from jax.sharding import PartitionSpec as P

NODE1D = 4
F32 = jnp.float32
BF16 = jnp.bfloat16
MESH = pl.DeviceIdType.MESH


def times(a, b):
    return lax.dot_general(a, b, (((1,), (0,)), ((), ())), preferred_element_type=F32)


def left_t(a, b):
    return lax.dot_general(a, b, (((0,), (0,)), ((), ())), preferred_element_type=F32)


def right_t(a, b):
    return lax.dot_general(a, b, (((1,), (1,)), ((), ())), preferred_element_type=F32)


def split(x):
    high = x.astype(BF16)
    return high, (x - high.astype(F32)).astype(BF16)


def pack(x):
    high, low = split(x)
    return jnp.concatenate([high, high, low], axis=0)


def stack(x):
    high, low = split(x)
    return jnp.concatenate([high, low, high], axis=0)


def merge(gathered, count):
    p = [gathered[i, 0:1] for i in range(count)]
    s = [gathered[i, 1:2] for i in range(count)]
    o = [gathered[i, 2:3] for i in range(count)]
    r = [gathered[i, 3:4] for i in range(count)]
    total = sum(s[1:], s[0])
    cross = sum((o[i] + p[i] * s[i] for i in range(1, count)), o[0] + p[0] * s[0])
    safe = jnp.where(total > 0.0, total, 1.0)
    common = jnp.where(total > 0.0, cross / safe, 0.0)
    odd = jnp.zeros_like(total)
    square = jnp.zeros_like(total)
    for i in range(count):
        shift = p[i] - common
        odd = odd + (o[i] + shift * s[i])
        square = square + (r[i] + shift * (2.0 * o[i] + shift * s[i]))
    return common, total, odd, square, cross


def kernel(
    sizes, lengths, north_of, vector, diagonal, lifting, inverse, xv, prod, coefs,
    dg, lf, iv, xs, top, bottom, south, north,
    below_in, above_in, west_in, east_in, at, mt, d, cf, ce, ck, cin, cpack, cout,
    stat1, all1, stat2, all2, final, final_in,
    in_sem, halo_send, halo_recv, chain_send, chain_recv,
    s1_send, s1_recv, s2_send, s2_recv, s3_send, s3_recv,
):
    lines, seg, block, face, cols, walls, surfs = sizes
    w = lax.axis_index("wall")
    s = lax.axis_index("surf")
    plane = NODE1D * NODE1D
    cube = plane * NODE1D
    outer = [0, lines - 1]
    inner = list(range(1, lines - 1))

    groups = [inner, outer[:1], outer[1:]]
    load_x = []
    for n, group in enumerate(groups):
        part = slice(group[0], group[-1] + 1)
        load_x.append(pltpu.make_async_copy(vector.at[part], xv.at[part], in_sem.at[0, n]))
    load_iv = pltpu.make_async_copy(inverse, iv, in_sem.at[3, 0])
    load_lf, load_dg = [], []
    for n, group in enumerate(groups):
        part = slice(group[0], group[-1] + 1)
        load_lf.append(
            pltpu.make_async_copy(lifting.at[part], lf.at[part], in_sem.at[1, n])
        )
        load_dg.append(
            pltpu.make_async_copy(diagonal.at[part], dg.at[part], in_sem.at[2, n])
        )
    for n in (1, 2, 0):
        load_x[n].start()
    load_iv.start()
    for copy in load_lf + load_dg:
        copy.start()
    barrier = pltpu.get_barrier_semaphore()
    for step in range(1, walls):
        pl.semaphore_signal(
            barrier, inc=1, device_id={"wall": lax.rem(w + step, walls)}, device_id_type=MESH
        )
    for step in range(1, surfs):
        pl.semaphore_signal(
            barrier, inc=1, device_id={"surf": lax.rem(s + step, surfs)}, device_id_type=MESH
        )

    def alive(l, k):
        return jnp.where(w * seg + k < lengths[l], 1.0, 0.0).astype(F32)

    def mask_line(l):
        def one(k, _):
            x = xv[l, k].astype(F32).reshape(block, cols) * alive(l, k)
            xv[l, k] = x.astype(BF16).reshape(xv.shape[2:])
            return 0

        lax.fori_loop(0, seg, one, 0, unroll=seg)

    load_x[1].wait()
    load_x[2].wait()
    for l in outer:
        mask_line(l)
    pl.semaphore_wait(barrier, walls - 1 + surfs - 1)

    def remote(src, dst, send, recv, target):
        return pltpu.make_async_remote_copy(
            src_ref=src, dst_ref=dst, send_sem=send, recv_sem=recv,
            device_id=target, device_id_type=MESH,
        )

    to_east = remote(
        xv.at[lines - 1, :, :, cube - plane:cube], west_in, halo_send.at[0], halo_recv.at[0],
        {"surf": lax.rem(s + 1, surfs)},
    )
    to_west = remote(
        xv.at[0, :, :, 0:plane], east_in, halo_send.at[1], halo_recv.at[1],
        {"surf": lax.rem(s + surfs - 1, surfs)},
    )
    to_east.start()
    to_west.start()
    load_x[0].wait()
    for l in inner:
        mask_line(l)

    count = block // plane

    def trace_one(l, k, i):
        x = xv[l, k].astype(F32).reshape(block, cols)
        slot = lax.rem(i, 4)
        for h in range(cols // 128):
            xs[slot, h] = x[:, h * 128:(h + 1) * 128]
        for h in range(cols // 128):
            at_h = pl.ds(h * 128, 128)
            bottom[l, k, :, at_h] = xs[slot, h, pl.ds(0, face, stride=NODE1D), :].astype(BF16)
            top[l, k + 1, :, at_h] = xs[
                slot, h, pl.ds(NODE1D - 1, face, stride=NODE1D), :
            ].astype(BF16)
        y = x.reshape(count, plane, cols)
        south[l, k] = y[:, 0:NODE1D].reshape(face, cols).astype(BF16)
        north[l, k] = y[:, plane - NODE1D:plane].reshape(face, cols).astype(BF16)

    def trace_ends(group, i, _):
        for l in group:
            trace_one(l, i * (seg - 1), 2 * i + group.index(l))
        return 0

    def trace_rest(i, _):
        trace_one(i // (seg - 2), 1 + i % (seg - 2), i)
        return 0


    up = {"wall": lax.rem(w + 1, walls)}
    down = {"wall": lax.rem(w + walls - 1, walls)}
    to_above, to_below = [], []
    for n, group in enumerate(groups):
        part = slice(group[0], group[-1] + 1)
        to_above.append(remote(
            top.at[part, seg], below_in.at[part], halo_send.at[2 + n], halo_recv.at[2 + n], up
        ))
        m = 2 + len(groups) + n
        to_below.append(remote(
            bottom.at[part, 0], above_in.at[part], halo_send.at[m], halo_recv.at[m], down
        ))

    def greet(parts):
        @pl.when(w < walls - 1)
        def _():
            for n in parts:
                to_above[n].start()

        @pl.when(w > 0)
        def _():
            for n in parts:
                to_below[n].start()

    lax.fori_loop(0, 2, functools.partial(trace_ends, inner), 0, unroll=2)
    greet([0])
    lax.fori_loop(0, 2, functools.partial(trace_ends, outer), 0, unroll=2)
    greet([1, 2])
    lax.fori_loop(0, lines * (seg - 2), trace_rest, 0, unroll=4)
    row = lax.broadcasted_iota(jnp.int32, (face, face), 0)
    column = lax.broadcasted_iota(jnp.int32, (face, face), 1)
    eye = jnp.where(row == column, 1.0, 0.0).astype(F32)

    def three(left, right):
        lh, ll = left[0:face], left[face:2 * face]
        rh, rl = right[0:face], right[face:2 * face]
        return times(lh, rh) + (times(ll, rh) + times(lh, rl))

    def map_one(group, k, _):
        for l in group:
            a = (-alive(l, k)) * right_t(lf[l, k, 0:face], iv[l, k])
            at[l, k] = stack(a)
        return 0

    load_iv.wait()
    for copy in load_lf:
        copy.wait()
    lax.fori_loop(0, seg, functools.partial(map_one, inner + outer), 0, unroll=4)

    @pl.when(w == 0)
    def _():
        mt[...] = jnp.zeros_like(mt)

    @pl.when(w > 0)
    def _():
        for l in range(lines):
            mt[l, 0] = stack(eye)
            mt[l, 1] = at[l, 0]
        for k in range(1, seg):
            for l in range(lines):
                mt[l, k + 1] = stack(three(mt[l, k], at[l, k]))

    south_of = []
    for l in range(lines):
        line = jnp.int32(0)
        for j in range(lines):
            line = jnp.where(north_of[0, j] == l, j, line)
        south_of.append(line)

    def fold(x):
        return jnp.sum(x.reshape(block // 8, 8, cols), axis=0)

    def local_step(group, k, acc):
        near, norm = acc
        for l in group:
            x = xv[l, k].reshape(block, cols)
            if l > 0:
                west = xv[l - 1, k, :, cube - plane:cube]
            else:
                west = west_in[k]
            if l < lines - 1:
                east = xv[l + 1, k, :, 0:plane]
            else:
                east = east_in[k]
            sides = [
                top[l, k], bottom[l, k + 1], west.reshape(face, cols), east.reshape(face, cols),
                north[south_of[l], k], south[north_of[0, l], k],
            ]
            p = times(dg[l, k], x) + left_t(lf[l, k], jnp.concatenate(sides, axis=0))
            p = alive(l, k) * p
            prod[l, k] = p
            wide = x.astype(F32)
            near = near + fold(wide * p)
            norm = norm + fold(wide * wide)
        return near, norm

    def inverse_step(group, k, _):
        for l in group:
            high, low = split(prod[l, k])
            d[l, k] = times(iv[l, k], high) + times(iv[l, k], low)
        return 0

    nothing = jnp.zeros((8, cols), F32)

    def meet(n):
        group = groups[n]

        @pl.when(w > 0)
        def _():
            to_above[n].wait_recv()
            for l in group:
                top[l, 0] = below_in[l]

        @pl.when(w == 0)
        def _():
            for l in group:
                top[l, 0] = jnp.zeros((face, cols), BF16)

        @pl.when(w < walls - 1)
        def _():
            to_below[n].wait_recv()
            for l in group:
                bottom[l, seg] = above_in[l]

        @pl.when(w == walls - 1)
        def _():
            for l in group:
                bottom[l, seg] = jnp.zeros((face, cols), BF16)

    chain = [
        remote(cout.at[l], cin.at[l], chain_send.at[l], chain_recv.at[l], up)
        for l in range(lines)
    ]

    def begin(group):
        @pl.when(w == 0)
        def _():
            for l in group:
                cout[l] = ce[l]
                chain[l].start()

    def take(group):
        for l in group:
            chain[l].wait_recv()
            cpack[l] = pack(cin[l])

            @pl.when(w < walls - 1)
            def _():
                cout[l] = ce[l] + left_t(mt[l, seg], cpack[l])
                chain[l].start()

    def process(n, acc):
        group = groups[n]
        load_dg[n].wait()
        once = 4
        meet(n)
        acc = lax.fori_loop(0, seg, functools.partial(local_step, group), acc, unroll=once)
        lax.fori_loop(0, seg, functools.partial(inverse_step, group), 0, unroll=seg)
        for l in group:
            cf[l, 0] = jnp.zeros((face, cols), F32)
            cf[l, 1] = d[l, 0]
        for k in range(1, seg):
            for l in group:
                c = d[l, k] + left_t(at[l, k], pack(cf[l, k]))
                if k < seg - 1:
                    cf[l, k + 1] = c
                else:
                    ce[l] = c
        begin(group)
        return acc

    @pl.when(w == 0)
    def _():
        cpack[...] = jnp.zeros_like(cpack)

    sums = process(0, (nothing, nothing))
    to_east.wait_recv()
    sums = process(1, sums)

    @pl.when(w == 1)
    def _():
        take(inner)

    to_west.wait_recv()
    near, norm = process(2, sums)

    @pl.when(w == 1)
    def _():
        take(outer)

    near = jnp.sum(near, axis=0, keepdims=True)
    norm = jnp.sum(norm, axis=0, keepdims=True)
    guess = jnp.where(norm > 0.0, near / jnp.where(norm > 0.0, norm, 1.0), 0.0)

    def carried(group, k, _):
        for l in group:
            c = (-alive(l, k)) * (cf[l, k] + left_t(mt[l, k], cpack[l]))
            high, low = split(c)
            ck[l, k, 0:face] = high
            ck[l, k, face:2 * face] = low
        return 0

    def correct_one(group, k, acc):
        odd, square = acc
        for l in group:
            lower = lf[l, k, 0:face]
            e = prod[l, k] + left_t(jnp.concatenate([lower, lower], axis=0), ck[l, k])
            prod[l, k] = e
            x = xv[l, k].astype(F32).reshape(block, cols)
            e = e - guess * x
            odd = odd + fold(x * e)
            square = square + fold(e * e)
        return odd, square

    def correct(group, acc):
        @pl.when(w > 1)
        def _():
            take(group)

        lax.fori_loop(0, seg, functools.partial(carried, group), 0, unroll=4)
        once = 4
        return lax.fori_loop(0, seg, functools.partial(correct_one, group), acc, unroll=once)

    sums = correct(inner, (nothing, nothing))
    sums = correct(outer[:1], sums)
    odd, square = correct(outer[1:], sums)
    odd = jnp.sum(odd, axis=0, keepdims=True)
    square = jnp.sum(square, axis=0, keepdims=True)

    last = walls - 1
    stat1[...] = jnp.concatenate(
        [guess, norm, odd, square], axis=0
    )

    def to_last(i):
        return remote(stat1, all1.at[i], s1_send.at[0], s1_recv.at[i], {"wall": last})

    def to_peer(step):
        return remote(
            stat2, all2.at[s], s2_send.at[step], s2_recv.at[step],
            {"surf": lax.rem(s + step, surfs)},
        )

    def to_wall(i):
        return remote(final, final_in, s3_send.at[i], s3_recv.at[0], {"wall": i})

    @pl.when(w < last)
    def _():
        to_last(w).start()
        to_wall(0).wait_recv()
        coefs[...] = final_in[...]
        to_last(w).wait_send()

    @pl.when(w == last)
    def _():
        for i in range(last):
            to_last(i).wait_recv()
        all1[last] = stat1[...]
        common, total, odd, square, _ = merge(all1, walls)
        block_of = jnp.concatenate(
            [common, total, odd, square], axis=0
        )
        stat2[...] = block_of
        all2[s] = block_of
        peers = [to_peer(step) for step in range(1, surfs)]
        for copy in peers:
            copy.start()
        for copy in peers:
            copy.wait_recv()
        _, total, _, square, cross = merge(all2, surfs)
        projection = cross / total
        entries = lines * seg * block * walls * surfs
        spread = jnp.sqrt(square / entries + 1e-06)
        result = jnp.concatenate([projection, spread], axis=0)
        final[...] = result
        for i in range(last):
            to_wall(i).start()
        coefs[...] = result
        for copy in peers:
            copy.wait_send()
        for i in range(last):
            to_wall(i).wait_send()

    to_east.wait_send()
    to_west.wait_send()

    @pl.when(w < walls - 1)
    def _():
        for copy in to_above:
            copy.wait_send()
        for copy in chain:
            copy.wait_send()

    @pl.when(w > 0)
    def _():
        for copy in to_below:
            copy.wait_send()


def finish(masked, eliminated, stats, basis, coefs):
    l = pl.program_id(0)
    coefs[...] = stats[...]
    projection = stats[0:1]
    scale = 1.0 / stats[1:2]
    pair = basis.shape[0]
    for h in range(pair):
        for k in range(basis.shape[1]):
            x = masked[pair * l + h, k].astype(F32).reshape(basis.shape[2:])
            basis[h, k] = ((eliminated[pair * l + h, k] - projection * x) * scale).astype(BF16)


def per_device(walls, surfs, vector, lengths, north_of, diagonal, lifting, inverse_rows):
    lines, seg, block, cols = vector.shape
    face = inverse_rows.shape[2]
    sizes = (lines, seg, block, face, cols, walls, surfs)
    stacked = lifting.reshape(lines, seg, lifting.shape[2] * face, block)
    smem = pl.BlockSpec(memory_space=pltpu.SMEM)
    vmem = pl.BlockSpec(memory_space=pltpu.VMEM)
    hbm = pl.BlockSpec(memory_space=pltpu.HBM)
    dma = pltpu.SemaphoreType.DMA
    cubes = (lines, seg, block // NODE1D**3, NODE1D**3, cols)
    slab = (seg, block // NODE1D**3, NODE1D**2, cols)
    masked, eliminated, stats = pl.pallas_call(
        functools.partial(kernel, sizes),
        out_shape=(
            pltpu.VMEM(cubes, BF16),
            pltpu.VMEM(vector.shape, F32),
            pltpu.VMEM((2, cols), F32),
        ),
        in_specs=[smem, smem, hbm, hbm, hbm, hbm],
        out_specs=(vmem, vmem, vmem),
        scratch_shapes=[
            pltpu.VMEM(diagonal.shape, BF16),
            pltpu.VMEM(stacked.shape, BF16),
            pltpu.VMEM(inverse_rows.shape, BF16),
            pltpu.VMEM((4, cols // 128, block, 128), F32),
            pltpu.VMEM((lines, seg + 1, face, cols), BF16),
            pltpu.VMEM((lines, seg + 1, face, cols), BF16),
            pltpu.VMEM((lines, seg, face, cols), BF16),
            pltpu.VMEM((lines, seg, face, cols), BF16),
            pltpu.VMEM((lines, face, cols), BF16),
            pltpu.VMEM((lines, face, cols), BF16),
            pltpu.VMEM(slab, BF16),
            pltpu.VMEM(slab, BF16),
            pltpu.VMEM((lines, seg, 3 * face, face), BF16),
            pltpu.VMEM((lines, seg + 1, 3 * face, face), BF16),
            pltpu.VMEM((lines, seg, face, cols), F32),
            pltpu.VMEM((lines, seg, face, cols), F32),
            pltpu.VMEM((lines, face, cols), F32),
            pltpu.VMEM((lines, seg, 2 * face, cols), BF16),
            pltpu.VMEM((lines, face, cols), F32),
            pltpu.VMEM((lines, 3 * face, cols), BF16),
            pltpu.VMEM((lines, face, cols), F32),
            pltpu.VMEM((4, cols), F32),
            pltpu.VMEM((walls, 4, cols), F32),
            pltpu.VMEM((4, cols), F32),
            pltpu.VMEM((surfs, 4, cols), F32),
            pltpu.VMEM((2, cols), F32),
            pltpu.VMEM((2, cols), F32),
            dma((4, 3)),
            dma((8,)),
            dma((8,)),
            dma((lines,)),
            dma((lines,)),
            dma((1,)),
            dma((walls,)),
            dma((surfs,)),
            dma((surfs,)),
            dma((walls,)),
            dma((1,)),
        ],
        compiler_params=pltpu.CompilerParams(
            collective_id=0, has_side_effects=True, vmem_limit_bytes=56 * 1024 * 1024
        ),
    )(lengths, north_of, vector.reshape(cubes), diagonal, stacked, inverse_rows)
    pair = 2 if lines % 2 == 0 else 1
    return pl.pallas_call(
        finish,
        grid=(lines // pair,),
        out_shape=(
            jax.ShapeDtypeStruct(vector.shape, BF16),
            jax.ShapeDtypeStruct((2, cols), F32),
        ),
        in_specs=[vmem, vmem, vmem],
        out_specs=(
            pl.BlockSpec((pair, seg, block, cols), lambda l: (l, 0, 0, 0)),
            pl.BlockSpec((2, cols), lambda l: (0, 0)),
        ),
        compiler_params=pltpu.CompilerParams(vmem_limit_bytes=16 * 1024 * 1024),
    )(masked, eliminated, stats)


def solution(mesh):
    in_specs = (
        P("surf", "wall", None, None),
        P("surf"),
        P("surf", None),
        P("surf", "wall", None, None),
        P("surf", "wall", None, None, None),
        P("surf", "wall", None, None),
    )
    out_specs = (P("surf", "wall", None, None), P())
    return jax.shard_map(
        functools.partial(per_device, mesh.shape["wall"], mesh.shape["surf"]),
        mesh=mesh, in_specs=in_specs, out_specs=out_specs, check_vma=False,
    )
```
